256 devices in a mesh: neur: 32 (over y, z_hi, core), tm: 8 (over x, z_lo).
Axes of the slice: x: 4, y: 4, z: 8 (z_hi: 4, z_lo: 2; z = z_hi * 2 + z_lo), core: 2. Of those that a mesh axis runs over, the one named last changes fastest.
Arguments:
- spikes: int32 [1024, 262144], P(None, ('neur', 'tm')), may hold values from 0 to 9
- held_in: int32 [262144], P(('neur', 'tm')), may hold values 0 or 1
- readin_weight: bfloat16 [262144, 1024], P(('neur', 'tm')), may hold values from -0.01171875 to 0.01171875
- qkv_weight: bfloat16 [1024, 3, 1024], P(None, None, 'tm'), may hold values from -0.1875 to 0.1875
- out_weight: bfloat16 [1024, 1024], P('tm'), may hold values from -0.1875 to 0.1875
- up_weight: bfloat16 [1024, 4096], P(None, 'tm'), may hold values from -0.1875 to 0.1875
- down_weight: bfloat16 [4096, 1024], P('tm'), may hold values from -0.09375 to 0.09375
- norm_gain: float32 [1024], replicated, may hold values from 0.25 to 1.75
- mlp_gain: float32 [1024], replicated, may hold values from 0.25 to 1.75
- final_gain: float32 [1024], replicated, may hold values from 0.25 to 1.75
- readout_weight: bfloat16 [262144, 1024], P(('neur', 'tm')), may hold values from -0.1875 to 0.1875
- readout_bias: float32 [262144], P(('neur', 'tm')), may hold values from -3 to 3
Outputs:
- latents: bfloat16 [1024, 1024], P('neur')
- neuron_bits: float32 [262144], P(('neur', 'tm'))
- bits_per_spike: float32 [], replicated
The draws below stay inside these ranges and needn't reach their ends.
All inputs are finite; a program needn't handle non-finite values. No bound on the sum of `held_in` on one device may be relied on, other than what follows from the above.
Results may differ from the reference program's by a relative error of at most 0.006.
Values may be sent and summed in bfloat16 or wider, within the bound.
No kernel may reach another device: no remote copies, remote signals or barrier semaphores. Data moves between devices by JAX's collectives and lax.ppermute only.
A program may use at most 64 MiB of HBM per device.

```python
import math
import jax
import jax.numpy as jnp
from jax import lax

D = 1024
HEADS = 8
HEAD_DIM = 128
FF = 4096
NEURONS = 262144
FRAMES = 1024
N_NEUR = 32


def draw_spikes(key, part):
    key_ceiling, key_counts = jax.random.split(key)
    column = jnp.arange(NEURONS, dtype=jnp.int32)
    ceiling = 3 + 6 * column // NEURONS + jax.random.randint(key_ceiling, (NEURONS,), 0, 3)
    return jax.random.randint(key_counts, (FRAMES, NEURONS), 0, ceiling[None, :]).astype(jnp.int32)


def touch_ends(values, key, least, high):
    longest = values.shape.index(max(values.shape))
    spots = []
    for shift in (0, 1):
        where = [jax.random.randint(jax.random.fold_in(key, axis), (), 0, length) for axis, length in enumerate(values.shape)]
        where[longest] = (where[longest] + shift) % values.shape[longest]
        spots.append(tuple(where))
    return values.at[spots[0]].set(least).at[spots[1]].set(high)


def steps_of(stream_key, extent, cuts, smallest, top_value):
    level = 1.0
    for axis_at, parts in cuts:
        draws = jax.random.uniform(jax.random.fold_in(jax.random.fold_in(stream_key, 6), axis_at), (parts,), jnp.float32, smallest / len(cuts), top_value / len(cuts))
        level = level * jnp.repeat(jnp.exp(draws), extent[axis_at] // parts).reshape((-1,) + (1,) * (len(extent) - 1 - axis_at))
    return level


def bell_draw(stream_key, extent, width, reach, pieces=(), held_as=jnp.bfloat16):
    values = jax.random.normal(stream_key, extent, jnp.float32) * width
    if len(pieces) > 0:
        values = steps_of(stream_key, extent, pieces, -0.22, 0.18) * values
    return jnp.clip(values, min=-reach, max=reach).astype(held_as)


def setup_inputs(seed: int = 0) -> dict:
    keys = jax.random.split(jax.random.key(seed), 13)
    return {
        "spikes": draw_spikes(jax.random.fold_in(keys[12], 71), 0),
        "held_in": touch_ends((jax.random.randint(keys[1], (NEURONS,), 0, 2) < 1).astype(jnp.int32), jax.random.fold_in(keys[1], 1), 0, 1),
        "readin_weight": bell_draw(keys[2], (NEURONS, D), NEURONS ** -0.5, 0.01171875, ((0, 256),)),
        "qkv_weight": bell_draw(keys[3], (D, 3, HEADS * HEAD_DIM), D ** -0.5, 0.1875, ((2, 8),)),
        "out_weight": bell_draw(keys[4], (HEADS * HEAD_DIM, D), (HEADS * HEAD_DIM) ** -0.5, 0.1875, ((0, 8),)),
        "up_weight": bell_draw(keys[5], (D, FF), D ** -0.5, 0.1875, ((1, 8),)),
        "down_weight": bell_draw(keys[6], (FF, D), FF ** -0.5, 0.09375, ((0, 8),)),
        "norm_gain": jnp.clip(1.0 + 0.15 * jax.random.normal(keys[7], (D,), jnp.float32), 0.25, 1.75),
        "mlp_gain": jnp.clip(1.0 + 0.15 * jax.random.normal(keys[8], (D,), jnp.float32), 0.25, 1.75),
        "final_gain": jnp.clip(1.0 + 0.15 * jax.random.normal(keys[9], (D,), jnp.float32), 0.25, 1.75),
        "readout_weight": bell_draw(keys[10], (NEURONS, D), D ** -0.5, 0.1875, ((0, 256),)),
        "readout_bias": bell_draw(keys[11], (NEURONS,), 0.5, 3.0, ((0, 256),), jnp.float32),
    }


def normed(values, gain_vec):
    return values * lax.rsqrt(lax.optimization_barrier(jnp.mean(values * values, -1, keepdims=True)) + 1e-05) * gain_vec

def reference(spikes, held_in, readin_weight, qkv_weight, out_weight, up_weight, down_weight, norm_gain, mlp_gain, final_gain, readout_weight, readout_bias):
    block_width = NEURONS // N_NEUR

    def readin_step(block_no, running):
        first_col = (block_no * block_width).astype(jnp.int32)
        cols = lax.dynamic_slice_in_dim(spikes, first_col, block_width, 1)
        mask_part = lax.dynamic_slice_in_dim(held_in, first_col, block_width, 0)
        masked = (cols * mask_part[None, :]).astype(jnp.bfloat16)
        rows_part = lax.dynamic_slice_in_dim(readin_weight, first_col, block_width, 0)
        return running + jnp.dot(masked, rows_part, preferred_element_type=jnp.float32)
    stream = lax.fori_loop(0, N_NEUR, readin_step, jnp.zeros((FRAMES, D), jnp.float32))
    attn_in = normed(stream, norm_gain).astype(jnp.bfloat16)
    head_cols = HEADS * HEAD_DIM
    projected = jnp.dot(attn_in, qkv_weight.reshape(D, 3 * head_cols), preferred_element_type=jnp.float32).astype(jnp.bfloat16)
    queries = projected[:, :head_cols].reshape(FRAMES, HEADS, HEAD_DIM).astype(jnp.float32)
    keys_all = projected[:, head_cols:2 * head_cols].reshape(FRAMES, HEADS, HEAD_DIM).astype(jnp.float32)
    values_all = projected[:, 2 * head_cols:].reshape(FRAMES, HEADS, HEAD_DIM).astype(jnp.float32)
    scores = jnp.einsum('qhd,khd->hqk', queries, keys_all) * (1.0 / math.sqrt(HEAD_DIM))
    weights = jnp.exp(scores)
    weights_low = weights.astype(jnp.bfloat16).astype(jnp.float32)
    numerator = jnp.einsum('hqk,khd->qhd', weights_low, values_all)
    denominator = lax.optimization_barrier(jnp.sum(weights, -1)).T
    heads_out = (numerator / denominator[:, :, None]).astype(jnp.bfloat16).reshape(FRAMES, head_cols)
    mixed_state = stream + jnp.dot(heads_out, out_weight, preferred_element_type=jnp.float32)
    mlp_in = normed(mixed_state, mlp_gain).astype(jnp.bfloat16)
    hidden_act = jax.nn.gelu(jnp.dot(mlp_in, up_weight, preferred_element_type=jnp.float32)).astype(jnp.bfloat16)
    final_state = mixed_state + jnp.dot(hidden_act, down_weight, preferred_element_type=jnp.float32)
    latents = normed(final_state, final_gain).astype(jnp.bfloat16)

    def readout_block(block_no):
        first_col = (block_no * block_width).astype(jnp.int32)
        rows_part = lax.dynamic_slice_in_dim(readout_weight, first_col, block_width, 0)
        bias_part = lax.dynamic_slice_in_dim(readout_bias, first_col, block_width, 0)
        observed = lax.dynamic_slice_in_dim(spikes, first_col, block_width, 1).astype(jnp.float32)
        log_rate = jnp.dot(latents, rows_part.T, preferred_element_type=jnp.float32) + bias_part[None, :]
        return lax.optimization_barrier(jnp.sum(observed * log_rate - jnp.exp(log_rate), 0))
    model_ll = lax.map(readout_block, jnp.arange(N_NEUR, dtype=jnp.int32)).reshape(NEURONS)
    counts = lax.optimization_barrier(jnp.sum(spikes, 0)).astype(jnp.float32)
    null_ll = counts * jnp.log((counts + 1.0) / FRAMES) - (counts + 1.0)
    heldout = (1 - held_in).astype(jnp.float32)
    gained = heldout * (model_ll - null_ll)
    neuron_bits = gained / (math.log(2.0) * (counts + 1.0))
    bits_per_spike = jnp.sum(gained) / (math.log(2.0) * (1.0 + jnp.sum(heldout * counts)))
    return (latents, neuron_bits, bits_per_spike)
```

```python
import math

import jax
import jax.numpy as jnp
from jax import lax
from jax.sharding import Mesh
from jax.sharding import PartitionSpec as P

HEAD_DIM = 128
BF16 = jnp.bfloat16
F32 = jnp.float32
ROWS = ("y", "zh", "c")
TM = ("x", "zl")
YZ = ("y", "zh")
CHIPS = ("y", "zh", "x", "zl")
ALL = ("y", "zh", "c", "x", "zl")


def normed(values, gain_vec):
    return values * lax.rsqrt(jnp.mean(values * values, -1, keepdims=True) + 1e-05) * gain_vec


def exchange(blocks, axes):
    return lax.all_to_all(blocks, axes, 0, 0, tiled=True)


def to_all(block, axes):
    return exchange(jnp.broadcast_to(block[None], (lax.axis_size(axes),) + block.shape), axes)


def other_core(block):
    return lax.ppermute(block, "c", [(0, 1), (1, 0)])


def on_device(
    spikes,
    held_in,
    readin_weight,
    qkv_weight,
    out_weight,
    up_weight,
    down_weight,
    norm_gain,
    mlp_gain,
    final_gain,
    readout_weight,
    readout_bias,
):
    frames_all = spikes.shape[0]
    model_dim = readin_weight.shape[1]
    chips = lax.axis_size(CHIPS)
    half = frames_all // 2
    rows_own = half // chips
    rows_here = frames_all // lax.axis_size(ROWS)
    core = lax.axis_index("c")

    def readin(start):
        block = lax.dynamic_slice_in_dim(spikes, start, half, 0)
        masked = (block * held_in[None, :]).astype(BF16)
        return jnp.dot(masked, readin_weight, preferred_element_type=F32)

    theirs = other_core(readin((1 - core) * half).astype(BF16))
    chip_sum = (readin(core * half) + theirs.astype(F32)).astype(BF16)
    parts = exchange(chip_sum.reshape(chips, rows_own, model_dim), CHIPS)
    own_rows = jnp.sum(parts.astype(F32), 0)
    stream = to_all(own_rows, TM).reshape(rows_here, model_dim)

    attn_in = normed(stream, norm_gain).astype(BF16)
    queries, keys, values = (
        jnp.dot(attn_in, qkv_weight[:, i], preferred_element_type=F32).astype(BF16)
        for i in range(3)
    )
    kv_near = to_all(jnp.concatenate([keys, values], 1), YZ).reshape(half, 2 * HEAD_DIM)
    kv_far = other_core(kv_near)
    numerator = 0.0
    denominator = 0.0
    for kv in (kv_near, kv_far):
        scores = lax.dot_general(
            queries, kv[:, :HEAD_DIM], (((1,), (1,)), ((), ())), preferred_element_type=F32
        )
        weights = jnp.exp(scores * (1.0 / math.sqrt(HEAD_DIM)))
        numerator += jnp.dot(weights.astype(BF16), kv[:, HEAD_DIM:], preferred_element_type=F32)
        denominator += jnp.sum(weights, -1, keepdims=True)
    heads_out = (numerator / denominator).astype(BF16)
    attn_part = jnp.dot(heads_out, out_weight, preferred_element_type=F32)
    mixed_state = stream + jnp.sum(to_all(attn_part.astype(BF16), TM).astype(F32), 0)

    mlp_in = normed(mixed_state, mlp_gain).astype(BF16)
    hidden_act = jax.nn.gelu(jnp.dot(mlp_in, up_weight, preferred_element_type=F32)).astype(BF16)
    mlp_part = jnp.dot(hidden_act, down_weight, preferred_element_type=F32)
    mlp_sum = jnp.sum(
        exchange(mlp_part.astype(BF16).reshape(-1, rows_own, model_dim), TM).astype(F32), 0
    )
    own_mixed = lax.dynamic_slice_in_dim(mixed_state, lax.axis_index(TM) * rows_own, rows_own, 0)
    own_latents = normed(own_mixed + mlp_sum, final_gain).astype(BF16)

    lat_near = to_all(own_latents, CHIPS).reshape(half, model_dim)
    lat_far = other_core(lat_near)
    model_ll = 0.0
    for lat, start in ((lat_near, core * half), (lat_far, (1 - core) * half)):
        log_rate = (
            lax.dot_general(
                lat, readout_weight, (((1,), (1,)), ((), ())), preferred_element_type=F32
            )
            + readout_bias[None, :]
        )
        observed = lax.dynamic_slice_in_dim(spikes, start, half, 0).astype(F32)
        model_ll += jnp.sum(observed * log_rate - jnp.exp(log_rate), 0)
    out_start = lax.axis_index(ROWS) * rows_here
    near = out_start // half == core
    out_row = lax.rem(out_start, half)
    latents = jnp.where(
        near,
        lax.dynamic_slice_in_dim(lat_near, out_row, rows_here, 0),
        lax.dynamic_slice_in_dim(lat_far, out_row, rows_here, 0),
    )

    heldout = (1 - held_in).astype(F32)
    counts = jnp.sum(spikes, 0).astype(F32)
    null_ll = counts * jnp.log((counts + 1.0) / frames_all) - (counts + 1.0)
    gained = heldout * (model_ll - null_ll)
    neuron_bits = gained / (math.log(2.0) * (counts + 1.0))
    sums = jnp.stack([jnp.sum(gained), jnp.sum(heldout * counts)])
    totals = jnp.sum(to_all(jnp.pad(sums, (0, 126))[None], ALL), (0, 1))
    bits_total = totals[0] / (math.log(2.0) * (1.0 + totals[1]))
    return (latents, neuron_bits, bits_total)


def solution(mesh):
    fine = Mesh(mesh.devices.reshape(4, 4, 2, 4, 2), ALL)
    in_specs = (
        P(None, ALL),
        P(ALL),
        P(ALL, None),
        P(None, None, TM),
        P(TM, None),
        P(None, TM),
        P(TM, None),
        P(),
        P(),
        P(),
        P(ALL, None),
        P(ALL),
    )
    out_specs = (P(ROWS, None), P(ALL), P())
    return jax.shard_map(
        on_device, mesh=fine, in_specs=in_specs, out_specs=out_specs, check_vma=False
    )
```

```python
import math

import jax
import jax.numpy as jnp
from jax import lax
from jax.sharding import Mesh
from jax.sharding import PartitionSpec as P

HEAD_DIM = 128
BF16 = jnp.bfloat16
F32 = jnp.float32
ROWS = ("y", "zh", "c")
TM = ("x", "zl")
YZ = ("y", "zh")
PLANE = ("y", "x")
COLUMN = ("x", "zh", "zl")
ALL = ("y", "zh", "c", "x", "zl")


def normed(values, gain_vec):
    return values * lax.rsqrt(jnp.mean(values * values, -1, keepdims=True) + 1e-05) * gain_vec


def exchange(blocks, axes):
    return lax.all_to_all(blocks, axes, 0, 0, tiled=True)


def to_all(block, axes):
    return exchange(jnp.broadcast_to(block[None], (lax.axis_size(axes),) + block.shape), axes)


def other_core(block):
    return lax.ppermute(block, "c", [(0, 1), (1, 0)])


def on_device(
    spikes,
    held_in,
    readin_weight,
    qkv_weight,
    out_weight,
    up_weight,
    down_weight,
    norm_gain,
    mlp_gain,
    final_gain,
    readout_weight,
    readout_bias,
):
    frames_all = spikes.shape[0]
    model_dim = readin_weight.shape[1]
    half = frames_all // 2
    rows_here = frames_all // lax.axis_size(ROWS)
    chunk = half // lax.axis_size("y")
    piece = chunk // (lax.axis_size("x") * lax.axis_size("zh"))
    core = lax.axis_index("c")
    y_at = lax.axis_index("y")

    def readin(start):
        block = lax.dynamic_slice_in_dim(spikes, start, half, 0)
        masked = (block * held_in[None, :]).astype(BF16)
        return jnp.dot(masked, readin_weight, preferred_element_type=F32)

    theirs = other_core(readin((1 - core) * half).astype(BF16))
    counts = jnp.sum(spikes, 0).astype(F32)
    theirs, counts = lax.optimization_barrier((theirs, counts))
    chip_sum = (readin(core * half) + theirs.astype(F32)).astype(BF16)
    plane_sum = jnp.sum(exchange(chip_sum.reshape(16, -1, model_dim), PLANE).astype(F32), 0)
    blocks = jnp.broadcast_to(
        plane_sum.astype(BF16).reshape(1, 4, 1, piece, model_dim), (4, 4, 2, piece, model_dim)
    )
    parts = exchange(blocks.reshape(32, piece, model_dim), COLUMN)
    stream = jnp.sum(parts.reshape(4, 8, piece, model_dim).astype(F32), 1)
    stream = stream.reshape(rows_here, model_dim)

    attn_in = normed(stream, norm_gain).astype(BF16)
    queries, keys, values = (
        jnp.dot(attn_in, qkv_weight[:, i], preferred_element_type=F32).astype(BF16)
        for i in range(3)
    )
    kv_near = to_all(jnp.concatenate([keys, values], 1), YZ).reshape(half, 2 * HEAD_DIM)
    kv_far = other_core(kv_near)
    numerator = 0.0
    denominator = 0.0
    for kv in (kv_near, kv_far):
        scores = lax.dot_general(
            queries, kv[:, :HEAD_DIM], (((1,), (1,)), ((), ())), preferred_element_type=F32
        )
        weights = jnp.exp(scores * (1.0 / math.sqrt(HEAD_DIM)))
        numerator += jnp.dot(weights.astype(BF16), kv[:, HEAD_DIM:], preferred_element_type=F32)
        denominator += jnp.sum(weights, -1, keepdims=True)
    heads_out = (numerator / denominator).astype(BF16)
    attn_part = jnp.dot(heads_out, out_weight, preferred_element_type=F32)
    mixed_state = stream + jnp.sum(to_all(attn_part.astype(BF16), TM).astype(F32), 0)

    mlp_in = normed(mixed_state, mlp_gain).astype(BF16)
    hidden_act = jax.nn.gelu(jnp.dot(mlp_in, up_weight, preferred_element_type=F32)).astype(BF16)
    mlp_part = jnp.dot(hidden_act, down_weight, preferred_element_type=F32)
    final_state = mixed_state + jnp.sum(to_all(mlp_part.astype(BF16), TM).astype(F32), 0)
    own_latents = normed(final_state, final_gain).astype(BF16)

    spread = to_all(own_latents.reshape(4, piece, model_dim), "zh")
    first = jnp.swapaxes(spread.reshape(4, 4, piece, model_dim), 0, 1).reshape(chunk, model_dim)
    near = [first] + [
        lax.ppermute(first, "y", [(i, (i + k) % 4) for i in range(4)]) for k in (1, 3, 2)
    ]
    chunks = []
    for lat, k in zip(near, (0, 1, 3, 2)):
        y_from = lax.rem(y_at + 4 - k, 4)
        chunks.append((lat, core, y_from))
        chunks.append((other_core(lat), 1 - core, y_from))
    out_start = lax.axis_index(ROWS) * rows_here
    out_chunk = out_start // chunk
    out_row = lax.rem(out_start, chunk)
    model_ll = 0.0
    latents = 0.0
    for lat, c_from, y_from in chunks:
        at = c_from * 4 + y_from
        log_rate = (
            lax.dot_general(
                lat, readout_weight, (((1,), (1,)), ((), ())), preferred_element_type=F32
            )
            + readout_bias[None, :]
        )
        observed = lax.dynamic_slice_in_dim(spikes, at * chunk, chunk, 0).astype(F32)
        model_ll += jnp.sum(observed * log_rate - jnp.exp(log_rate), 0)
        rows = lax.dynamic_slice_in_dim(lat, out_row, rows_here, 0)
        latents += jnp.where(at == out_chunk, rows, jnp.zeros_like(rows))

    heldout = (1 - held_in).astype(F32)
    null_ll = counts * jnp.log((counts + 1.0) / frames_all) - (counts + 1.0)
    gained = heldout * (model_ll - null_ll)
    neuron_bits = gained / (math.log(2.0) * (counts + 1.0))
    sums = jnp.stack([jnp.sum(gained), jnp.sum(heldout * counts)])
    totals = jnp.sum(to_all(jnp.pad(sums, (0, 126))[None], ALL), (0, 1))
    bits_total = totals[0] / (math.log(2.0) * (1.0 + totals[1]))
    return (latents, neuron_bits, bits_total)


def solution(mesh):
    fine = Mesh(mesh.devices.reshape(4, 4, 2, 4, 2), ALL)
    in_specs = (
        P(None, ALL),
        P(ALL),
        P(ALL, None),
        P(None, None, TM),
        P(TM, None),
        P(None, TM),
        P(TM, None),
        P(),
        P(),
        P(),
        P(ALL, None),
        P(ALL),
    )
    out_specs = (P(ROWS, None), P(ALL), P())
    return jax.shard_map(
        on_device, mesh=fine, in_specs=in_specs, out_specs=out_specs, check_vma=False
    )
```

```python
import math

import jax
import jax.numpy as jnp
from jax import lax
from jax.sharding import Mesh
from jax.sharding import PartitionSpec as P

HEAD_DIM = 128
BF16 = jnp.bfloat16
F32 = jnp.float32
ROWS = ("y", "zh", "c")
TM = ("x", "zl")
PLANE = ("y", "x")
ALL = ("y", "zh", "c", "x", "zl")


def normed(values, gain_vec):
    return values * lax.rsqrt(jnp.mean(values * values, -1, keepdims=True) + 1e-05) * gain_vec


def exchange(blocks, axes):
    return lax.all_to_all(blocks, axes, 0, 0, tiled=True)


def to_all(block, axes):
    return exchange(jnp.broadcast_to(block[None], (lax.axis_size(axes),) + block.shape), axes)


def other_core(block):
    return lax.ppermute(block, "c", [(0, 1), (1, 0)])


def on_device(
    spikes,
    held_in,
    readin_weight,
    qkv_weight,
    out_weight,
    up_weight,
    down_weight,
    norm_gain,
    mlp_gain,
    final_gain,
    readout_weight,
    readout_bias,
):
    frames_all = spikes.shape[0]
    model_dim = readin_weight.shape[1]
    half = frames_all // 2
    rows_here = frames_all // lax.axis_size(ROWS)
    chunk = half // lax.axis_size("y")
    core = lax.axis_index("c")
    y_at = lax.axis_index("y")

    def readin(start):
        block = lax.dynamic_slice_in_dim(spikes, start, half, 0)
        masked = (block * held_in[None, :]).astype(BF16)
        return jnp.dot(masked, readin_weight, preferred_element_type=F32)

    theirs = other_core(readin((1 - core) * half).astype(BF16))
    counts = jnp.sum(spikes, 0).astype(F32)
    theirs, counts = lax.optimization_barrier((theirs, counts))
    chip_sum = (readin(core * half) + theirs.astype(F32)).astype(BF16)
    plane_sum = jnp.sum(exchange(chip_sum.reshape(16, -1, model_dim), PLANE).astype(F32), 0)
    stream = jnp.sum(to_all(plane_sum.astype(BF16), ("zh", "zl")).astype(F32), 0)

    attn_own = normed(stream, norm_gain).astype(BF16)
    attn_near = to_all(attn_own, PLANE).reshape(half, model_dim)
    attn_far = other_core(attn_near)

    def project(frames, part):
        return jnp.dot(frames, qkv_weight[:, part], preferred_element_type=F32).astype(BF16)

    own_start = y_at * chunk + lax.axis_index("zh") * rows_here
    queries = project(lax.dynamic_slice_in_dim(attn_near, own_start, rows_here, 0), 0)
    numerator = 0.0
    denominator = 0.0
    for frames in (attn_near, attn_far):
        scores = lax.dot_general(
            queries, project(frames, 1), (((1,), (1,)), ((), ())), preferred_element_type=F32
        )
        weights = jnp.exp(scores * (1.0 / math.sqrt(HEAD_DIM)))
        numerator += jnp.dot(
            weights.astype(BF16), project(frames, 2), preferred_element_type=F32
        )
        denominator += jnp.sum(weights, -1, keepdims=True)
    heads_out = (numerator / denominator).astype(BF16)
    attn_part = jnp.dot(heads_out, out_weight, preferred_element_type=F32)
    holder = (lax.axis_index("x") == lax.axis_index("zh")) & (lax.axis_index("zl") == 0)
    attn_part += jnp.where(holder, stream, jnp.zeros_like(stream))
    mixed_state = jnp.sum(to_all(attn_part.astype(BF16), TM).astype(F32), 0)

    mlp_in = normed(mixed_state, mlp_gain).astype(BF16)
    hidden_act = jax.nn.gelu(jnp.dot(mlp_in, up_weight, preferred_element_type=F32)).astype(BF16)
    mlp_part = jnp.dot(hidden_act, down_weight, preferred_element_type=F32)
    final_state = mixed_state + jnp.sum(to_all(mlp_part.astype(BF16), TM).astype(F32), 0)
    own_latents = normed(final_state, final_gain).astype(BF16)

    first = to_all(own_latents, "zh").reshape(chunk, model_dim)
    near = [first] + [
        lax.ppermute(first, "y", [(i, (i + k) % 4) for i in range(4)]) for k in (1, 3, 2)
    ]
    chunks = []
    for lat, k in zip(near, (0, 1, 3, 2)):
        y_from = lax.rem(y_at + 4 - k, 4)
        chunks.append((lat, core, y_from))
        chunks.append((other_core(lat), 1 - core, y_from))
    out_start = lax.axis_index(ROWS) * rows_here
    out_chunk = out_start // chunk
    out_row = lax.rem(out_start, chunk)
    model_ll = 0.0
    latents = 0.0
    for lat, c_from, y_from in chunks:
        at = c_from * 4 + y_from
        log_rate = (
            lax.dot_general(
                lat, readout_weight, (((1,), (1,)), ((), ())), preferred_element_type=F32
            )
            + readout_bias[None, :]
        )
        observed = lax.dynamic_slice_in_dim(spikes, at * chunk, chunk, 0).astype(F32)
        model_ll += jnp.sum(observed * log_rate - jnp.exp(log_rate), 0)
        rows = lax.dynamic_slice_in_dim(lat, out_row, rows_here, 0)
        latents += jnp.where(at == out_chunk, rows, jnp.zeros_like(rows))

    heldout = (1 - held_in).astype(F32)
    null_ll = counts * jnp.log((counts + 1.0) / frames_all) - (counts + 1.0)
    gained = heldout * (model_ll - null_ll)
    neuron_bits = gained / (math.log(2.0) * (counts + 1.0))
    sums = jnp.stack([jnp.sum(gained), jnp.sum(heldout * counts)])
    totals = jnp.sum(to_all(jnp.pad(sums, (0, 126))[None], ALL), (0, 1))
    bits_total = totals[0] / (math.log(2.0) * (1.0 + totals[1]))
    return (latents, neuron_bits, bits_total)


def solution(mesh):
    fine = Mesh(mesh.devices.reshape(4, 4, 2, 4, 2), ALL)
    in_specs = (
        P(None, ALL),
        P(ALL),
        P(ALL, None),
        P(None, None, TM),
        P(TM, None),
        P(None, TM),
        P(TM, None),
        P(),
        P(),
        P(),
        P(ALL, None),
        P(ALL),
    )
    out_specs = (P(ROWS, None), P(ALL), P())
    return jax.shard_map(
        on_device, mesh=fine, in_specs=in_specs, out_specs=out_specs, check_vma=False
    )
```

```python
import functools
import math

import jax
import jax.numpy as jnp
from jax import lax
from jax.experimental import pallas as pl
from jax.experimental.pallas import tpu as pltpu
from jax.sharding import Mesh
from jax.sharding import PartitionSpec as P

HEAD_DIM = 128
BF16 = jnp.bfloat16
F32 = jnp.float32
ROWS = ("y", "zh", "c")
TM = ("x", "zl")
PLANE = ("y", "x")
ALL = ("y", "zh", "c", "x", "zl")


def normed(values, gain_vec):
    return values * lax.rsqrt(jnp.mean(values * values, -1, keepdims=True) + 1e-05) * gain_vec


def exchange(blocks, axes):
    return lax.all_to_all(blocks, axes, 0, 0, tiled=True)


def to_all(block, axes):
    return exchange(jnp.broadcast_to(block[None], (lax.axis_size(axes),) + block.shape), axes)


def other_core(block):
    return lax.ppermute(block, "c", [(0, 1), (1, 0)])


def whole(array):
    return pl.BlockSpec(array.shape, lambda *_: (0,) * array.ndim)


def in_hbm(array):
    return pltpu.with_memory_space_constraint(array, pltpu.HBM)


def params(semantics):
    return pltpu.CompilerParams(
        dimension_semantics=semantics, vmem_limit_bytes=40 * 1024 * 1024
    )


def matmul(left, right):
    return jnp.dot(left, right, preferred_element_type=F32)


def matmul_nt(left, right):
    return lax.dot_general(left, right, (((1,), (1,)), ((), ())), preferred_element_type=F32)


def readin_kernel(at_ref, spikes_ref, held_ref, weight_ref, out_ref, counts_ref):
    block = spikes_ref[...]
    masked = (block * held_ref[...]).astype(F32).astype(BF16)
    out_ref[...] = matmul(masked, weight_ref[...]).astype(out_ref.dtype)
    counted = jnp.sum(block.astype(F32), 0, keepdims=True)

    @pl.when(pl.program_id(0) == 0)
    def _():
        counts_ref[...] = counted

    @pl.when(pl.program_id(0) > 0)
    def _():
        counts_ref[...] += counted


def readin(spikes, held, weight, which_half, dtype):
    frames, neurons = spikes.shape
    dim = weight.shape[1]
    rows = frames // 4
    return pl.pallas_call(
        readin_kernel,
        out_shape=(
            jax.ShapeDtypeStruct((frames // 2, dim), dtype),
            jax.ShapeDtypeStruct((1, neurons), F32),
        ),
        grid_spec=pltpu.PrefetchScalarGridSpec(
            num_scalar_prefetch=1,
            grid=(2,),
            in_specs=[
                pl.BlockSpec((rows, neurons), lambda i, at: (2 * at[0] + i, 0)),
                pl.BlockSpec((1, neurons), lambda i, at: (0, 0)),
                pl.BlockSpec((neurons, dim), lambda i, at: (0, 0)),
            ],
            out_specs=[
                pl.BlockSpec((rows, dim), lambda i, at: (i, 0)),
                pl.BlockSpec((1, neurons), lambda i, at: (0, 0)),
            ],
        ),
        compiler_params=params(("arbitrary",)),
        cost_estimate=pl.CostEstimate(
            flops=frames * neurons * dim,
            bytes_accessed=2 * frames * neurons + 2 * neurons * dim + frames * dim,
            transcendentals=0,
        ),
        name="readin",
    )(which_half.reshape(1), in_hbm(spikes), held, in_hbm(weight))


def attend(queries, frames_ref, weight_ref):
    frames = frames_ref[...]
    keys = matmul(frames, weight_ref[1]).astype(BF16)
    values = matmul(frames, weight_ref[2]).astype(BF16)
    weights = jnp.exp(matmul_nt(queries, keys) * (1.0 / math.sqrt(HEAD_DIM)))
    return matmul(weights.astype(BF16), values), jnp.sum(weights, -1, keepdims=True)


def attend_near_kernel(at_ref, frames_ref, weight_ref, queries_ref, num_ref, den_ref):
    rows = queries_ref.shape[0]
    own = frames_ref[pl.ds(pl.multiple_of(at_ref[0] * rows, rows), rows), :]
    queries = matmul(own, weight_ref[0]).astype(BF16)
    queries_ref[...] = queries
    numerator, denominator = attend(queries, frames_ref, weight_ref)
    num_ref[...] = numerator
    den_ref[...] = jnp.broadcast_to(denominator, den_ref.shape)


def attend_near(frames, weight, block_at, rows):
    smem = pl.BlockSpec(memory_space=pltpu.SMEM)
    shape = (rows, HEAD_DIM)
    return pl.pallas_call(
        attend_near_kernel,
        out_shape=(
            jax.ShapeDtypeStruct(shape, BF16),
            jax.ShapeDtypeStruct(shape, F32),
            jax.ShapeDtypeStruct(shape, F32),
        ),
        in_specs=[smem, whole(frames), whole(weight)],
        out_specs=[pl.BlockSpec(shape, lambda: (0, 0))] * 3,
        compiler_params=params(None),
        cost_estimate=pl.CostEstimate(
            flops=4 * frames.shape[0] * frames.shape[1] * HEAD_DIM,
            bytes_accessed=2 * frames.size,
            transcendentals=rows * frames.shape[0],
        ),
        name="attend_near",
    )(block_at.reshape(1), frames, weight)


def attend_far_kernel(
    holder_ref, frames_ref, weight_ref, queries_ref, num_ref, den_ref, mix_ref, stream_ref, out_ref
):
    numerator, denominator = attend(queries_ref[...], frames_ref, weight_ref)
    heads_out = ((num_ref[...] + numerator) / (den_ref[...] + denominator)).astype(BF16)
    held = jnp.where(holder_ref[0] == 1, stream_ref[...], jnp.zeros_like(stream_ref))
    part = (matmul(heads_out, mix_ref[...]) + held).astype(BF16)
    for i in range(out_ref.shape[0]):
        out_ref[i] = part


def attend_far(holder, frames, weight, queries, numerator, denominator, mix, stream, copies):
    smem = pl.BlockSpec(memory_space=pltpu.SMEM)
    shape = (copies,) + stream.shape
    operands = (frames, weight, queries, numerator, denominator, mix, stream)
    return pl.pallas_call(
        attend_far_kernel,
        out_shape=jax.ShapeDtypeStruct(shape, BF16),
        in_specs=[smem] + [whole(array) for array in operands],
        out_specs=pl.BlockSpec(shape, lambda: (0, 0, 0)),
        compiler_params=params(None),
        cost_estimate=pl.CostEstimate(
            flops=4 * frames.shape[0] * frames.shape[1] * HEAD_DIM,
            bytes_accessed=2 * frames.size,
            transcendentals=stream.shape[0] * frames.shape[0],
        ),
        name="attend_far",
    )(holder.reshape(1), *operands)


def score_kernel(frames, near_ref, far_ref, held_ref, seen_ref, seen_too_ref, bits_ref, sums_ref):
    heldout = (1 - held_ref[...]).astype(F32)
    count = seen_ref[...] + seen_too_ref[...]
    null_ll = count * jnp.log((count + 1.0) / frames) - (count + 1.0)
    gained = heldout * (near_ref[...] + far_ref[...] - null_ll)
    bits_ref[...] = gained / (math.log(2.0) * (count + 1.0))
    lane = lax.broadcasted_iota(jnp.int32, (1, 128), 1)
    gain_sum = jnp.sum(gained, 1, keepdims=True)
    spike_sum = jnp.sum(heldout * count, 1, keepdims=True)
    here = jnp.where(lane == 0, gain_sum, jnp.where(lane == 1, spike_sum, 0.0))
    sums_ref[...] = jnp.broadcast_to(here[None], sums_ref.shape)


def score(frames, copies, *rows):
    shape = (copies, 1, 128)
    return pl.pallas_call(
        functools.partial(score_kernel, float(frames)),
        out_shape=(
            jax.ShapeDtypeStruct(rows[0].shape, F32),
            jax.ShapeDtypeStruct(shape, F32),
        ),
        in_specs=[whole(row) for row in rows],
        out_specs=[whole(rows[0]), pl.BlockSpec(shape, lambda: (0, 0, 0))],
        name="score",
    )(*rows)


def on_device(
    spikes,
    held_in,
    readin_weight,
    qkv_weight,
    out_weight,
    up_weight,
    down_weight,
    norm_gain,
    mlp_gain,
    final_gain,
    readout_weight,
    readout_bias,
):
    frames_all = spikes.shape[0]
    model_dim = readin_weight.shape[1]
    half = frames_all // 2
    rows_here = frames_all // lax.axis_size(ROWS)
    chunk = half // lax.axis_size("y")
    core = lax.axis_index("c")
    y_at = lax.axis_index("y")
    held_row = held_in[None, :]

    given, counts_far = readin(spikes, held_row, readin_weight, 1 - core, BF16)
    theirs = other_core(given)
    own, counts_near = readin(spikes, held_row, readin_weight, core, F32)
    chip_sum = (own + theirs.astype(F32)).astype(BF16)
    plane_sum = jnp.sum(exchange(chip_sum.reshape(16, -1, model_dim), PLANE).astype(F32), 0)
    stream = jnp.sum(to_all(plane_sum.astype(BF16), ("zh", "zl")).astype(F32), 0)

    attn_own = normed(stream, norm_gain).astype(BF16)
    attn_near = to_all(attn_own, PLANE).reshape(half, model_dim)
    attn_far = other_core(attn_near)
    qkv = jnp.swapaxes(qkv_weight, 0, 1)
    own_block = y_at * lax.axis_size("zh") + lax.axis_index("zh")
    queries, numerator, denominator = attend_near(attn_near, qkv, own_block, rows_here)
    holder = (lax.axis_index("x") == lax.axis_index("zh")) & (lax.axis_index("zl") == 0)
    parts = attend_far(
        holder.astype(jnp.int32), attn_far, qkv, queries, numerator, denominator,
        out_weight, stream, lax.axis_size(TM),
    )
    mixed_state = jnp.sum(exchange(parts, TM).astype(F32), 0)

    mlp_in = normed(mixed_state, mlp_gain).astype(BF16)
    hidden_act = jax.nn.gelu(jnp.dot(mlp_in, up_weight, preferred_element_type=F32)).astype(BF16)
    mlp_part = jnp.dot(hidden_act, down_weight, preferred_element_type=F32)
    final_state = mixed_state + jnp.sum(to_all(mlp_part.astype(BF16), TM).astype(F32), 0)
    own_latents = normed(final_state, final_gain).astype(BF16)

    mine = to_all(own_latents, "zh").reshape(chunk, model_dim)
    lat_near = to_all(mine, "y").reshape(half, model_dim)
    lat_far = other_core(lat_near)

    def likelihood(lat, start):
        log_rate = matmul_nt(lat, readout_weight) + readout_bias[None, :]
        observed = lax.dynamic_slice_in_dim(spikes, start, half, 0).astype(F32)
        return jnp.sum(observed * log_rate - jnp.exp(log_rate), 0, keepdims=True)

    bits, sums = score(
        frames_all, lax.axis_size(ALL),
        likelihood(lat_near, core * half), likelihood(lat_far, (1 - core) * half),
        held_row, counts_near, counts_far,
    )
    totals = jnp.sum(exchange(sums, ALL), (0, 1))
    bits_total = totals[0] / (math.log(2.0) * (1.0 + totals[1]))

    out_start = lax.axis_index(ROWS) * rows_here
    out_row = lax.rem(out_start, half)
    latents = jnp.where(
        out_start // half == core,
        lax.dynamic_slice_in_dim(lat_near, out_row, rows_here, 0),
        lax.dynamic_slice_in_dim(lat_far, out_row, rows_here, 0),
    )
    return (latents, bits[0], bits_total)


def solution(mesh):
    fine = Mesh(mesh.devices.reshape(4, 4, 2, 4, 2), ALL)
    in_specs = (
        P(None, ALL),
        P(ALL),
        P(ALL, None),
        P(None, None, TM),
        P(TM, None),
        P(None, TM),
        P(TM, None),
        P(),
        P(),
        P(),
        P(ALL, None),
        P(ALL),
    )
    out_specs = (P(ROWS, None), P(ALL), P())
    return jax.shard_map(
        on_device, mesh=fine, in_specs=in_specs, out_specs=out_specs, check_vma=False
    )
```

```python
import functools
import math

import jax
import jax.numpy as jnp
from jax import lax
from jax.experimental import pallas as pl
from jax.experimental.pallas import tpu as pltpu
from jax.sharding import Mesh
from jax.sharding import PartitionSpec as P

HEAD_DIM = 128
BF16 = jnp.bfloat16
F32 = jnp.float32
ROWS = ("y", "zh", "c")
TM = ("x", "zl")
PLANE = ("y", "x")
YZ = ("y", "zh")
ALL = ("y", "zh", "c", "x", "zl")


def normed(values, gain_vec):
    return values * lax.rsqrt(jnp.mean(values * values, -1, keepdims=True) + 1e-05) * gain_vec


def exchange(blocks, axes):
    return lax.all_to_all(blocks, axes, 0, 0, tiled=True)


def to_all(block, axes):
    return exchange(jnp.broadcast_to(block[None], (lax.axis_size(axes),) + block.shape), axes)


def other_core(block):
    return lax.ppermute(block, "c", [(0, 1), (1, 0)])


def other_layer(block):
    return lax.ppermute(block, "zl", [(0, 1), (1, 0)])


def whole(array):
    return pl.BlockSpec(array.shape, lambda *_: (0,) * array.ndim)


def in_hbm(array):
    return pltpu.with_memory_space_constraint(array, pltpu.HBM)


def params(semantics):
    return pltpu.CompilerParams(
        dimension_semantics=semantics, vmem_limit_bytes=40 * 1024 * 1024
    )


def matmul(left, right):
    return jnp.dot(left, right, preferred_element_type=F32)


def matmul_nt(left, right):
    return lax.dot_general(left, right, (((1,), (1,)), ((), ())), preferred_element_type=F32)


def readin_kernel(at_ref, spikes_ref, held_ref, weight_ref, out_ref, counts_ref, total):
    step = pl.program_id(0)
    block = spikes_ref[...]
    masked = (block * held_ref[...]).astype(F32).astype(BF16)
    product = matmul(masked, weight_ref[...])
    counts_ref[...] = jnp.sum(block.astype(F32), 0, keepdims=True)

    @pl.when(step == 0)
    def _():
        total[...] = product

    @pl.when(step > 0)
    def _():
        total[...] += product

    @pl.when(step == pl.num_programs(0) - 1)
    def _():
        out_ref[...] = total[...].astype(out_ref.dtype)


def readin(spikes, held, weight, which_half, dtype):
    frames, neurons = spikes.shape
    dim = weight.shape[1]
    rows, width = frames // 2, neurons // 4
    return pl.pallas_call(
        readin_kernel,
        out_shape=(
            jax.ShapeDtypeStruct((rows, dim), dtype),
            jax.ShapeDtypeStruct((1, neurons), F32),
        ),
        grid_spec=pltpu.PrefetchScalarGridSpec(
            num_scalar_prefetch=1,
            grid=(4,),
            in_specs=[
                pl.BlockSpec((rows, width), lambda k, at: (at[0], k)),
                pl.BlockSpec((1, width), lambda k, at: (0, k)),
                pl.BlockSpec((width, dim), lambda k, at: (k, 0)),
            ],
            out_specs=[
                pl.BlockSpec((rows, dim), lambda k, at: (0, 0)),
                pl.BlockSpec((1, width), lambda k, at: (0, k)),
            ],
            scratch_shapes=[pltpu.VMEM((rows, dim), F32)],
        ),
        compiler_params=params(("arbitrary",)),
        cost_estimate=pl.CostEstimate(
            flops=frames * neurons * dim,
            bytes_accessed=2 * frames * neurons + 2 * neurons * dim + frames * dim,
            transcendentals=0,
        ),
        name="readin",
    )(which_half.reshape(1), in_hbm(spikes), held, in_hbm(weight))


def project_kernel(parts_ref, gain_ref, weight_ref, stream_ref, queries_ref, kv_ref):
    groups = parts_ref.shape[0] // 4
    piece = parts_ref.shape[1]
    for x in range(4):
        rows = parts_ref[groups * x].astype(F32)
        for i in range(1, groups):
            rows += parts_ref[groups * x + i].astype(F32)
        stream_ref[piece * x : piece * (x + 1), :] = rows
    attn_in = normed(stream_ref[...], gain_ref[...]).astype(BF16)
    queries_ref[...] = matmul(attn_in, weight_ref[0]).astype(BF16)
    keys = matmul(attn_in, weight_ref[1]).astype(BF16)
    values = matmul(attn_in, weight_ref[2]).astype(BF16)
    for i in range(kv_ref.shape[0]):
        kv_ref[i, :, :HEAD_DIM] = keys
        kv_ref[i, :, HEAD_DIM:] = values


def project(parts, gain, weight, copies):
    rows, dim = 4 * parts.shape[1], parts.shape[2]
    shapes = ((rows, dim), F32), ((rows, HEAD_DIM), BF16), ((copies, rows, 2 * HEAD_DIM), BF16)
    return pl.pallas_call(
        project_kernel,
        out_shape=[jax.ShapeDtypeStruct(*shape) for shape in shapes],
        in_specs=[whole(array) for array in (parts, gain, weight)],
        out_specs=[
            pl.BlockSpec(shape, lambda n=len(shape): (0,) * n) for shape, _ in shapes
        ],
        compiler_params=params(None),
        name="project",
    )(parts, gain, weight)


def attend_kernel(queries_ref, near_ref, far_ref, mix_ref, out_ref):
    queries = queries_ref[...]
    numerator, denominator = 0.0, 0.0
    for kv in (near_ref, far_ref):
        scores = matmul_nt(queries, kv[:, :HEAD_DIM])
        weights = jnp.exp(scores * (1.0 / math.sqrt(HEAD_DIM)))
        numerator += matmul(weights.astype(BF16), kv[:, HEAD_DIM:])
        denominator += jnp.sum(weights, -1, keepdims=True)
    part = matmul((numerator / denominator).astype(BF16), mix_ref[...]).astype(BF16)
    for i in range(out_ref.shape[0]):
        out_ref[i] = part


def attend(queries, near, far, mix, copies):
    shape = (copies, queries.shape[0], mix.shape[1])
    operands = (queries, near, far, mix)
    return pl.pallas_call(
        attend_kernel,
        out_shape=jax.ShapeDtypeStruct(shape, BF16),
        in_specs=[whole(array) for array in operands],
        out_specs=pl.BlockSpec(shape, lambda: (0, 0, 0)),
        compiler_params=params(None),
        name="attend",
    )(*operands)


def score_kernel(frames, near_ref, far_ref, held_ref, seen_ref, seen_too_ref, bits_ref, sums_ref):
    heldout = (1 - held_ref[...]).astype(F32)
    count = seen_ref[...] + seen_too_ref[...]
    null_ll = count * jnp.log((count + 1.0) / frames) - (count + 1.0)
    gained = heldout * (near_ref[...] + far_ref[...] - null_ll)
    bits_ref[...] = gained / (math.log(2.0) * (count + 1.0))
    lane = lax.broadcasted_iota(jnp.int32, (1, 128), 1)
    gain_sum = jnp.sum(gained, 1, keepdims=True)
    spike_sum = jnp.sum(heldout * count, 1, keepdims=True)
    here = jnp.where(lane == 0, gain_sum, jnp.where(lane == 1, spike_sum, 0.0))
    sums_ref[...] = jnp.broadcast_to(here[None], sums_ref.shape)


def score(frames, copies, *rows):
    shape = (copies, 1, 128)
    return pl.pallas_call(
        functools.partial(score_kernel, float(frames)),
        out_shape=(
            jax.ShapeDtypeStruct(rows[0].shape, F32),
            jax.ShapeDtypeStruct(shape, F32),
        ),
        in_specs=[whole(row) for row in rows],
        out_specs=[whole(rows[0]), pl.BlockSpec(shape, lambda: (0, 0, 0))],
        name="score",
    )(*rows)


def on_device(
    spikes,
    held_in,
    readin_weight,
    qkv_weight,
    out_weight,
    up_weight,
    down_weight,
    norm_gain,
    mlp_gain,
    final_gain,
    readout_weight,
    readout_bias,
):
    frames_all = spikes.shape[0]
    model_dim = readin_weight.shape[1]
    half = frames_all // 2
    rows_here = frames_all // lax.axis_size(ROWS)
    core = lax.axis_index("c")
    held_row = held_in[None, :]

    given, counts_far = readin(spikes, held_row, readin_weight, 1 - core, BF16)
    theirs = other_core(given)
    own, counts_near = readin(spikes, held_row, readin_weight, core, F32)
    chip_sum = (own + theirs.astype(F32)).astype(BF16)
    plane_sum = jnp.sum(exchange(chip_sum.reshape(16, -1, model_dim), PLANE).astype(F32), 0)
    plane_sum = plane_sum.astype(BF16)
    pair_sum = (plane_sum.astype(F32) + other_layer(plane_sum).astype(F32)).astype(BF16)
    blocks = jnp.broadcast_to(pair_sum.reshape(1, 4, -1, model_dim), (4, 4, 8, model_dim))
    parts = exchange(blocks.reshape(16, 8, model_dim), ("x", "zh"))

    stream, queries, kv_own = project(
        parts, norm_gain[None, :], jnp.swapaxes(qkv_weight, 0, 1), lax.axis_size(YZ)
    )
    kv_near = exchange(kv_own, YZ).reshape(half, 2 * HEAD_DIM)
    attn_parts = attend(queries, kv_near, other_core(kv_near), out_weight, lax.axis_size(TM))
    mixed_state = stream + jnp.sum(exchange(attn_parts, TM).astype(F32), 0)

    mlp_in = normed(mixed_state, mlp_gain).astype(BF16)
    hidden_act = jax.nn.gelu(jnp.dot(mlp_in, up_weight, preferred_element_type=F32)).astype(BF16)
    mlp_part = jnp.dot(hidden_act, down_weight, preferred_element_type=F32)
    mlp_sum = jnp.sum(
        exchange(mlp_part.astype(BF16).reshape(8, -1, model_dim), TM).astype(F32), 0
    )
    rows_own = mlp_sum.shape[0]
    own_mixed = lax.dynamic_slice_in_dim(mixed_state, lax.axis_index(TM) * rows_own, rows_own, 0)
    own_latents = normed(own_mixed + mlp_sum, final_gain).astype(BF16)

    column = to_all(own_latents, ("zh", "zl")).reshape(rows_here, model_dim)
    lat_near = to_all(column, PLANE).reshape(half, model_dim)
    lat_far = other_core(lat_near)

    def likelihood(lat, start):
        log_rate = matmul_nt(lat, readout_weight) + readout_bias[None, :]
        observed = lax.dynamic_slice_in_dim(spikes, start, half, 0).astype(F32)
        return jnp.sum(observed * log_rate - jnp.exp(log_rate), 0, keepdims=True)

    bits, sums = score(
        frames_all, lax.axis_size(ALL),
        likelihood(lat_near, core * half), likelihood(lat_far, (1 - core) * half),
        held_row, counts_near, counts_far,
    )
    totals = jnp.sum(exchange(sums, ALL), (0, 1))
    bits_total = totals[0] / (math.log(2.0) * (1.0 + totals[1]))

    out_start = lax.axis_index(ROWS) * rows_here
    out_row = lax.rem(out_start, half)
    latents = jnp.where(
        out_start // half == core,
        lax.dynamic_slice_in_dim(lat_near, out_row, rows_here, 0),
        lax.dynamic_slice_in_dim(lat_far, out_row, rows_here, 0),
    )
    return (latents, bits[0], bits_total)


def solution(mesh):
    fine = Mesh(mesh.devices.reshape(4, 4, 2, 4, 2), ALL)
    in_specs = (
        P(None, ALL),
        P(ALL),
        P(ALL, None),
        P(None, None, TM),
        P(TM, None),
        P(None, TM),
        P(TM, None),
        P(),
        P(),
        P(),
        P(ALL, None),
        P(ALL),
    )
    out_specs = (P(ROWS, None), P(ALL), P())
    return jax.shard_map(
        on_device, mesh=fine, in_specs=in_specs, out_specs=out_specs, check_vma=False
    )
```

```python
import functools
import math

import jax
import jax.numpy as jnp
from jax import lax
from jax.experimental import pallas as pl
from jax.experimental.pallas import tpu as pltpu
from jax.sharding import Mesh
from jax.sharding import PartitionSpec as P

HEAD_DIM = 128
BF16 = jnp.bfloat16
F32 = jnp.float32
ROWS = ("y", "zh", "c")
TM = ("x", "zl")
PLANE = ("y", "x")
YZ = ("y", "zh")
ALL = ("y", "zh", "c", "x", "zl")


def normed(values, gain_vec):
    return values * lax.rsqrt(jnp.mean(values * values, -1, keepdims=True) + 1e-05) * gain_vec


def exchange(blocks, axes):
    return lax.all_to_all(blocks, axes, 0, 0, tiled=True)


def to_all(block, axes):
    return exchange(jnp.broadcast_to(block[None], (lax.axis_size(axes),) + block.shape), axes)


def other_core(block):
    return lax.ppermute(block, "c", [(0, 1), (1, 0)])


def other_layer(block):
    return lax.ppermute(block, "zl", [(0, 1), (1, 0)])


def whole(array):
    return pl.BlockSpec(array.shape, lambda *_: (0,) * array.ndim)


def in_hbm(array):
    return pltpu.with_memory_space_constraint(array, pltpu.HBM)


def params(semantics):
    return pltpu.CompilerParams(
        dimension_semantics=semantics, vmem_limit_bytes=40 * 1024 * 1024
    )


def matmul(left, right):
    return jnp.dot(left, right, preferred_element_type=F32)


def matmul_nt(left, right):
    return lax.dot_general(left, right, (((1,), (1,)), ((), ())), preferred_element_type=F32)


def readin_kernel(at_ref, spikes_ref, held_ref, weight_ref, out_ref, counts_ref):
    block = spikes_ref[...]
    masked = (block * held_ref[...]).astype(F32).astype(BF16)
    out_ref[...] = matmul(masked, weight_ref[...]).astype(out_ref.dtype)
    counted = jnp.sum(block.astype(F32), 0, keepdims=True)

    @pl.when(pl.program_id(0) == 0)
    def _():
        counts_ref[...] = counted

    @pl.when(pl.program_id(0) > 0)
    def _():
        counts_ref[...] += counted


def readin(spikes, held, weight, which_half, dtype):
    frames, neurons = spikes.shape
    dim = weight.shape[1]
    rows = frames // 4
    return pl.pallas_call(
        readin_kernel,
        out_shape=(
            jax.ShapeDtypeStruct((frames // 2, dim), dtype),
            jax.ShapeDtypeStruct((1, neurons), F32),
        ),
        grid_spec=pltpu.PrefetchScalarGridSpec(
            num_scalar_prefetch=1,
            grid=(2,),
            in_specs=[
                pl.BlockSpec((rows, neurons), lambda i, at: (2 * at[0] + i, 0)),
                pl.BlockSpec((1, neurons), lambda i, at: (0, 0)),
                pl.BlockSpec((neurons, dim), lambda i, at: (0, 0)),
            ],
            out_specs=[
                pl.BlockSpec((rows, dim), lambda i, at: (i, 0)),
                pl.BlockSpec((1, neurons), lambda i, at: (0, 0)),
            ],
        ),
        compiler_params=params(("arbitrary",)),
        cost_estimate=pl.CostEstimate(
            flops=frames * neurons * dim,
            bytes_accessed=2 * frames * neurons + 2 * neurons * dim + frames * dim,
            transcendentals=0,
        ),
        name="readin",
    )(which_half.reshape(1), in_hbm(spikes), in_hbm(held), in_hbm(weight))


def plane_kernel(parts_ref, out_ref):
    total = parts_ref[0].astype(F32)
    for i in range(1, parts_ref.shape[0]):
        total += parts_ref[i].astype(F32)
    out_ref[...] = total.astype(BF16)


def pair_kernel(mine_ref, other_ref, out_ref):
    total = (mine_ref[...].astype(F32) + other_ref[...].astype(F32)).astype(BF16)
    piece = out_ref.shape[1]
    for i in range(out_ref.shape[0]):
        start = piece * (i % 4)
        out_ref[i] = total[start : start + piece]


def small(body, name, out_shapes, *operands, scalar=None):
    specs = [whole(array) for array in operands]
    if scalar is not None:
        specs.insert(0, pl.BlockSpec(memory_space=pltpu.SMEM))
        operands = (scalar.reshape(1),) + operands
    return pl.pallas_call(
        body,
        out_shape=[jax.ShapeDtypeStruct(*shape) for shape in out_shapes],
        in_specs=specs,
        out_specs=[
            pl.BlockSpec(shape, lambda n=len(shape): (0,) * n) for shape, _ in out_shapes
        ],
        compiler_params=params(None),
        name=name,
    )(*operands)


def mlp_kernel(parts_ref, stream_ref, gain_ref, up_ref, down_ref, mixed_ref, out_ref):
    mixed = stream_ref[...]
    attn = parts_ref[0].astype(F32)
    for i in range(1, parts_ref.shape[0]):
        attn += parts_ref[i].astype(F32)
    mixed += attn
    mlp_in = normed(mixed, gain_ref[...]).astype(BF16)
    hidden_act = jax.nn.gelu(matmul(mlp_in, up_ref[...])).astype(BF16)
    part = matmul(hidden_act, down_ref[...])
    rows = out_ref.shape[1]
    for i in range(out_ref.shape[0]):
        mixed_ref[i] = mixed[rows * i : rows * (i + 1)]
        out_ref[i] = part[rows * i : rows * (i + 1)].astype(BF16)


def latents_kernel(at_ref, parts_ref, mixed_ref, gain_ref, out_ref):
    total = parts_ref[0].astype(F32)
    for i in range(1, parts_ref.shape[0]):
        total += parts_ref[i].astype(F32)
    own = normed(mixed_ref[at_ref[0]] + total, gain_ref[...]).astype(BF16)
    for i in range(out_ref.shape[0]):
        out_ref[i] = own


def project_kernel(parts_ref, gain_ref, weight_ref, stream_ref, queries_ref, kv_ref):
    groups = parts_ref.shape[0] // 4
    piece = parts_ref.shape[1]
    for x in range(4):
        rows = parts_ref[groups * x].astype(F32)
        for i in range(1, groups):
            rows += parts_ref[groups * x + i].astype(F32)
        stream_ref[piece * x : piece * (x + 1), :] = rows
    attn_in = normed(stream_ref[...], gain_ref[...]).astype(BF16)
    queries_ref[...] = matmul(attn_in, weight_ref[0]).astype(BF16)
    keys = matmul(attn_in, weight_ref[1]).astype(BF16)
    values = matmul(attn_in, weight_ref[2]).astype(BF16)
    for i in range(kv_ref.shape[0]):
        kv_ref[i, :, :HEAD_DIM] = keys
        kv_ref[i, :, HEAD_DIM:] = values


def project(parts, gain, weight, copies):
    rows, dim = 4 * parts.shape[1], parts.shape[2]
    shapes = ((rows, dim), F32), ((rows, HEAD_DIM), BF16), ((copies, rows, 2 * HEAD_DIM), BF16)
    return pl.pallas_call(
        project_kernel,
        out_shape=[jax.ShapeDtypeStruct(*shape) for shape in shapes],
        in_specs=[whole(array) for array in (parts, gain, weight)],
        out_specs=[
            pl.BlockSpec(shape, lambda n=len(shape): (0,) * n) for shape, _ in shapes
        ],
        compiler_params=params(None),
        name="project",
    )(parts, gain, weight)


def attend_kernel(queries_ref, near_ref, far_ref, mix_ref, out_ref):
    queries = queries_ref[...]
    numerator, denominator = 0.0, 0.0
    for kv in (near_ref, far_ref):
        scores = matmul_nt(queries, kv[:, :HEAD_DIM])
        weights = jnp.exp(scores * (1.0 / math.sqrt(HEAD_DIM)))
        numerator += matmul(weights.astype(BF16), kv[:, HEAD_DIM:])
        denominator += jnp.sum(weights, -1, keepdims=True)
    part = matmul((numerator / denominator).astype(BF16), mix_ref[...]).astype(BF16)
    for i in range(out_ref.shape[0]):
        out_ref[i] = part


def attend(queries, near, far, mix, copies):
    shape = (copies, queries.shape[0], mix.shape[1])
    operands = (queries, near, far, mix)
    return pl.pallas_call(
        attend_kernel,
        out_shape=jax.ShapeDtypeStruct(shape, BF16),
        in_specs=[whole(array) for array in operands],
        out_specs=pl.BlockSpec(shape, lambda: (0, 0, 0)),
        compiler_params=params(None),
        name="attend",
    )(*operands)


def likelihood(lat_ref, spikes_ref, weight_ref, bias_ref):
    log_rate = matmul_nt(lat_ref[...], weight_ref[...]) + bias_ref[...]
    observed = spikes_ref[...].astype(F32)
    return jnp.sum(observed * log_rate - jnp.exp(log_rate), 0, keepdims=True)


def readout_kernel(at_ref, lat, spikes, weight, bias, out):
    out[...] = likelihood(lat, spikes, weight, bias)


def score_kernel(
    frames, at_ref, lat, spikes, weight, bias, before, held, seen, seen_too, bits, sums, total
):
    step = pl.program_id(0)
    model_ll = before[...] + likelihood(lat, spikes, weight, bias)
    heldout = (1 - held[...]).astype(F32)
    count = seen[...] + seen_too[...]
    null_ll = count * jnp.log((count + 1.0) / frames) - (count + 1.0)
    gained = heldout * (model_ll - null_ll)
    bits[...] = gained / (math.log(2.0) * (count + 1.0))
    lane = lax.broadcasted_iota(jnp.int32, (1, 128), 1)
    gain_sum = jnp.sum(gained, 1, keepdims=True)
    spike_sum = jnp.sum(heldout * count, 1, keepdims=True)
    here = jnp.where(lane == 0, gain_sum, jnp.where(lane == 1, spike_sum, 0.0))

    @pl.when(step == 0)
    def _():
        total[...] = here

    @pl.when(step > 0)
    def _():
        total[...] += here

    @pl.when(step == pl.num_programs(0) - 1)
    def _():
        sums[...] = jnp.broadcast_to(total[...][None], sums.shape)


def readout(which_half, lat, spikes, weight, bias, scoring=(), copies=256):
    frames, neurons = spikes.shape
    rows, dim = lat.shape
    width = neurons // 4
    row = pl.BlockSpec((1, width), lambda j, at: (0, j))
    out_shape, out_specs = [jax.ShapeDtypeStruct((1, neurons), F32)], [row]
    body, scratch = readout_kernel, []
    if scoring:
        body = functools.partial(score_kernel, float(frames))
        out_shape.append(jax.ShapeDtypeStruct((copies, 1, 128), F32))
        out_specs.append(pl.BlockSpec((copies, 1, 128), lambda j, at: (0, 0, 0)))
        scratch = [pltpu.VMEM((1, 128), F32)]
    return pl.pallas_call(
        body,
        out_shape=out_shape,
        grid_spec=pltpu.PrefetchScalarGridSpec(
            num_scalar_prefetch=1,
            grid=(neurons // width,),
            in_specs=[
                pl.BlockSpec((rows, dim), lambda j, at: (0, 0)),
                pl.BlockSpec((rows, width), lambda j, at: (at[0], j)),
                pl.BlockSpec((width, dim), lambda j, at: (j, 0)),
            ]
            + [row] * (1 + len(scoring)),
            out_specs=out_specs,
            scratch_shapes=scratch,
        ),
        compiler_params=params(("arbitrary",)),
        cost_estimate=pl.CostEstimate(
            flops=2 * rows * dim * neurons,
            bytes_accessed=4 * rows * neurons + 2 * weight.size,
            transcendentals=rows * neurons,
        ),
        name="score" if scoring else "readout",
    )(which_half.reshape(1), lat, in_hbm(spikes), weight, bias, *scoring)


def on_device(
    spikes,
    held_in,
    readin_weight,
    qkv_weight,
    out_weight,
    up_weight,
    down_weight,
    norm_gain,
    mlp_gain,
    final_gain,
    readout_weight,
    readout_bias,
):
    frames_all = spikes.shape[0]
    model_dim = readin_weight.shape[1]
    half = frames_all // 2
    rows_here = frames_all // lax.axis_size(ROWS)
    core = lax.axis_index("c")
    held_row = held_in[None, :]

    given, counts_far = readin(spikes, held_row, readin_weight, 1 - core, BF16)
    theirs = other_core(given)
    own, counts_near = readin(spikes, held_row, readin_weight, core, F32)
    chip_sum = (own + theirs.astype(F32)).astype(BF16)
    wide = ((rows_here, model_dim), BF16)
    (plane_sum,) = small(
        plane_kernel, "plane", [wide], exchange(chip_sum.reshape(16, -1, model_dim), PLANE)
    )
    (blocks,) = small(
        pair_kernel, "pair", [((16, rows_here // 4, model_dim), BF16)],
        plane_sum, other_layer(plane_sum),
    )
    parts = exchange(blocks, ("x", "zh"))

    stream, queries, kv_own = project(
        parts, norm_gain[None, :], jnp.swapaxes(qkv_weight, 0, 1), lax.axis_size(YZ)
    )
    kv_near = exchange(kv_own, YZ).reshape(half, 2 * HEAD_DIM)
    attn_parts = attend(queries, kv_near, other_core(kv_near), out_weight, lax.axis_size(TM))

    thin = (8, rows_here // 8, model_dim)
    mixed, mlp_parts = small(
        mlp_kernel, "mlp", [(thin, F32), (thin, BF16)],
        exchange(attn_parts, TM), stream, mlp_gain[None, :], up_weight, down_weight,
    )
    (own_latents,) = small(
        latents_kernel, "latents", [(thin, BF16)],
        exchange(mlp_parts, TM), mixed, final_gain[None, :], scalar=lax.axis_index(TM),
    )

    column = exchange(own_latents, ("zh", "zl")).reshape(rows_here, model_dim)
    lat_near = to_all(column, PLANE).reshape(half, model_dim)
    lat_far = other_core(lat_near)

    bias_row = readout_bias[None, :]
    (ll_near,) = readout(core, lat_near, spikes, readout_weight, bias_row)
    scoring = (ll_near, held_row, counts_near, counts_far)
    bits, sums = readout(1 - core, lat_far, spikes, readout_weight, bias_row, scoring)
    totals = jnp.sum(exchange(sums, ALL), (0, 1))
    bits_total = totals[0] / (math.log(2.0) * (1.0 + totals[1]))

    out_start = lax.axis_index(ROWS) * rows_here
    out_row = lax.rem(out_start, half)
    latents = jnp.where(
        out_start // half == core,
        lax.dynamic_slice_in_dim(lat_near, out_row, rows_here, 0),
        lax.dynamic_slice_in_dim(lat_far, out_row, rows_here, 0),
    )
    return (latents, bits[0], bits_total)


def solution(mesh):
    fine = Mesh(mesh.devices.reshape(4, 4, 2, 4, 2), ALL)
    in_specs = (
        P(None, ALL),
        P(ALL),
        P(ALL, None),
        P(None, None, TM),
        P(TM, None),
        P(None, TM),
        P(TM, None),
        P(),
        P(),
        P(),
        P(ALL, None),
        P(ALL),
    )
    out_specs = (P(ROWS, None), P(ALL), P())
    return jax.shard_map(
        on_device, mesh=fine, in_specs=in_specs, out_specs=out_specs, check_vma=False
    )
```

```python
import functools
import math

import jax
import jax.numpy as jnp
from jax import lax
from jax.experimental import pallas as pl
from jax.experimental.pallas import tpu as pltpu
from jax.sharding import Mesh
from jax.sharding import PartitionSpec as P

HEAD_DIM = 128
BF16 = jnp.bfloat16
F32 = jnp.float32
ROWS = ("y", "zh", "c")
TM = ("x", "zl")
PLANE = ("y", "x")
YZ = ("y", "zh")
ALL = ("y", "zh", "c", "x", "zl")


def normed(values, gain_vec):
    return values * lax.rsqrt(jnp.mean(values * values, -1, keepdims=True) + 1e-05) * gain_vec


def exchange(blocks, axes):
    return lax.all_to_all(blocks, axes, 0, 0, tiled=True)


def to_all(block, axes):
    return exchange(jnp.broadcast_to(block[None], (lax.axis_size(axes),) + block.shape), axes)


def other_core(block):
    return lax.ppermute(block, "c", [(0, 1), (1, 0)])


def other_layer(block):
    return lax.ppermute(block, "zl", [(0, 1), (1, 0)])


def whole(array):
    return pl.BlockSpec(array.shape, lambda *_: (0,) * array.ndim)


def in_hbm(array):
    return pltpu.with_memory_space_constraint(array, pltpu.HBM)


def params(semantics):
    return pltpu.CompilerParams(
        dimension_semantics=semantics, vmem_limit_bytes=40 * 1024 * 1024
    )


def matmul(left, right):
    return jnp.dot(left, right, preferred_element_type=F32)


def matmul_nt(left, right):
    return lax.dot_general(left, right, (((1,), (1,)), ((), ())), preferred_element_type=F32)


def readin_kernel(at_ref, spikes_ref, held_ref, weight_ref, out_ref, counts_ref):
    block = spikes_ref[...]
    masked = (block * held_ref[...]).astype(F32).astype(BF16)
    out_ref[...] = matmul(masked, weight_ref[...]).astype(out_ref.dtype)
    counted = jnp.sum(block.astype(F32), 0, keepdims=True)

    @pl.when(pl.program_id(0) == 0)
    def _():
        counts_ref[...] = counted

    @pl.when(pl.program_id(0) > 0)
    def _():
        counts_ref[...] += counted


def readin(spikes, held, weight, which_half, dtype):
    frames, neurons = spikes.shape
    dim = weight.shape[1]
    rows = frames // 4
    return pl.pallas_call(
        readin_kernel,
        out_shape=(
            jax.ShapeDtypeStruct((frames // 2, dim), dtype),
            jax.ShapeDtypeStruct((1, neurons), F32),
        ),
        grid_spec=pltpu.PrefetchScalarGridSpec(
            num_scalar_prefetch=1,
            grid=(2,),
            in_specs=[
                pl.BlockSpec((rows, neurons), lambda i, at: (2 * at[0] + i, 0)),
                pl.BlockSpec((1, neurons), lambda i, at: (0, 0)),
                pl.BlockSpec((neurons, dim), lambda i, at: (0, 0)),
            ],
            out_specs=[
                pl.BlockSpec((rows, dim), lambda i, at: (i, 0)),
                pl.BlockSpec((1, neurons), lambda i, at: (0, 0)),
            ],
        ),
        compiler_params=params(("arbitrary",)),
        cost_estimate=pl.CostEstimate(
            flops=frames * neurons * dim,
            bytes_accessed=2 * frames * neurons + 2 * neurons * dim + frames * dim,
            transcendentals=0,
        ),
        name="readin",
    )(which_half.reshape(1), in_hbm(spikes), in_hbm(held), weight)


def plane_kernel(parts_ref, out_ref):
    total = parts_ref[0].astype(F32)
    for i in range(1, parts_ref.shape[0]):
        total += parts_ref[i].astype(F32)
    out_ref[...] = total.astype(BF16)


def pair_kernel(mine_ref, other_ref, out_ref):
    total = (mine_ref[...].astype(F32) + other_ref[...].astype(F32)).astype(BF16)
    piece = out_ref.shape[1]
    for i in range(out_ref.shape[0]):
        start = piece * (i % 4)
        out_ref[i] = total[start : start + piece]


def small(body, name, out_shapes, *operands, scalar=None):
    specs = [whole(array) for array in operands]
    if scalar is not None:
        specs.insert(0, pl.BlockSpec(memory_space=pltpu.SMEM))
        operands = (scalar.reshape(1),) + operands
    return pl.pallas_call(
        body,
        out_shape=[jax.ShapeDtypeStruct(*shape) for shape in out_shapes],
        in_specs=specs,
        out_specs=[
            pl.BlockSpec(shape, lambda n=len(shape): (0,) * n) for shape, _ in out_shapes
        ],
        compiler_params=params(None),
        name=name,
    )(*operands)


def mlp_kernel(parts_ref, stream_ref, gain_ref, up_ref, down_ref, mixed_ref, out_ref):
    mixed = stream_ref[...]
    attn = parts_ref[0].astype(F32)
    for i in range(1, parts_ref.shape[0]):
        attn += parts_ref[i].astype(F32)
    mixed += attn
    mlp_in = normed(mixed, gain_ref[...]).astype(BF16)
    hidden_act = jax.nn.gelu(matmul(mlp_in, up_ref[...])).astype(BF16)
    part = matmul(hidden_act, down_ref[...])
    rows = out_ref.shape[1]
    for i in range(out_ref.shape[0]):
        mixed_ref[i] = mixed[rows * i : rows * (i + 1)]
        out_ref[i] = part[rows * i : rows * (i + 1)].astype(BF16)


def latents_kernel(at_ref, parts_ref, mixed_ref, gain_ref, out_ref):
    total = parts_ref[0].astype(F32)
    for i in range(1, parts_ref.shape[0]):
        total += parts_ref[i].astype(F32)
    own = normed(mixed_ref[at_ref[0]] + total, gain_ref[...]).astype(BF16)
    for i in range(out_ref.shape[0]):
        out_ref[i] = own


def project_kernel(parts_ref, gain_ref, weight_ref, stream_ref, queries_ref, kv_ref):
    groups = parts_ref.shape[0] // 4
    piece = parts_ref.shape[1]
    for x in range(4):
        rows = parts_ref[groups * x].astype(F32)
        for i in range(1, groups):
            rows += parts_ref[groups * x + i].astype(F32)
        stream_ref[piece * x : piece * (x + 1), :] = rows
    attn_in = normed(stream_ref[...], gain_ref[...]).astype(BF16)
    queries_ref[...] = matmul(attn_in, weight_ref[0]).astype(BF16)
    keys = matmul(attn_in, weight_ref[1]).astype(BF16)
    values = matmul(attn_in, weight_ref[2]).astype(BF16)
    for i in range(kv_ref.shape[0]):
        kv_ref[i, :, :HEAD_DIM] = keys
        kv_ref[i, :, HEAD_DIM:] = values


def project(parts, gain, weight, copies):
    rows, dim = 4 * parts.shape[1], parts.shape[2]
    shapes = ((rows, dim), F32), ((rows, HEAD_DIM), BF16), ((copies, rows, 2 * HEAD_DIM), BF16)
    return pl.pallas_call(
        project_kernel,
        out_shape=[jax.ShapeDtypeStruct(*shape) for shape in shapes],
        in_specs=[whole(array) for array in (parts, gain, weight)],
        out_specs=[
            pl.BlockSpec(shape, lambda n=len(shape): (0,) * n) for shape, _ in shapes
        ],
        compiler_params=params(None),
        name="project",
    )(parts, gain, weight)


def attend_kernel(queries_ref, near_ref, far_ref, mix_ref, out_ref):
    queries = queries_ref[...]
    numerator, denominator = 0.0, 0.0
    for kv in (near_ref, far_ref):
        scores = matmul_nt(queries, kv[:, :HEAD_DIM])
        weights = jnp.exp(scores * (1.0 / math.sqrt(HEAD_DIM)))
        numerator += matmul(weights.astype(BF16), kv[:, HEAD_DIM:])
        denominator += jnp.sum(weights, -1, keepdims=True)
    part = matmul((numerator / denominator).astype(BF16), mix_ref[...]).astype(BF16)
    for i in range(out_ref.shape[0]):
        out_ref[i] = part


def attend(queries, near, far, mix, copies):
    shape = (copies, queries.shape[0], mix.shape[1])
    operands = (queries, near, far, mix)
    return pl.pallas_call(
        attend_kernel,
        out_shape=jax.ShapeDtypeStruct(shape, BF16),
        in_specs=[whole(array) for array in operands],
        out_specs=pl.BlockSpec(shape, lambda: (0, 0, 0)),
        compiler_params=params(None),
        name="attend",
    )(*operands)


def likelihood(lat_ref, spikes_ref, weight_ref, bias_ref):
    log_rate = matmul_nt(lat_ref[...], weight_ref[...]) + bias_ref[...]
    observed = spikes_ref[...].astype(F32)
    return jnp.sum(observed * log_rate - jnp.exp(log_rate), 0, keepdims=True)


def readout_kernel(at_ref, lat, spikes, weight, bias, out):
    out[...] = likelihood(lat, spikes, weight, bias)


def score_kernel(
    frames, at_ref, lat, spikes, weight, bias, before, held, seen, seen_too, bits, sums, total
):
    step = pl.program_id(0)
    width = spikes.shape[1]
    found = likelihood(lat, spikes, weight, bias)
    for j in range(total.shape[1] // width):

        @pl.when(step == j)
        def _():
            total[:, width * j : width * (j + 1)] = found

    @pl.when(step == pl.num_programs(0) - 1)
    def _():
        heldout = (1 - held[...]).astype(F32)
        count = seen[...] + seen_too[...]
        null_ll = count * jnp.log((count + 1.0) / frames) - (count + 1.0)
        gained = heldout * (before[...] + total[...] - null_ll)
        bits[...] = gained / (math.log(2.0) * (count + 1.0))
        lane = lax.broadcasted_iota(jnp.int32, (1, 128), 1)
        gain_sum = jnp.sum(gained, 1, keepdims=True)
        spike_sum = jnp.sum(heldout * count, 1, keepdims=True)
        here = jnp.where(lane == 0, gain_sum, jnp.where(lane == 1, spike_sum, 0.0))
        sums[...] = jnp.broadcast_to(here[None], sums.shape)


def total_kernel(sums_ref, out_ref):
    totals = jnp.sum(sums_ref[...], 0)
    out_ref[...] = totals[:, 0:1] / (math.log(2.0) * (1.0 + totals[:, 1:2]))


def readout(which_half, lat, spikes, weight, bias, scoring=(), copies=256):
    frames, neurons = spikes.shape
    rows, dim = lat.shape
    width = neurons // 2
    row = pl.BlockSpec((1, width), lambda j, at: (0, j))
    out_shape, out_specs = [jax.ShapeDtypeStruct((1, neurons), F32)], [row]
    body, scratch = readout_kernel, []
    if scoring:
        body = functools.partial(score_kernel, float(frames))
        out_shape.append(jax.ShapeDtypeStruct((copies, 1, 128), F32))
        out_specs = [
            pl.BlockSpec((1, neurons), lambda j, at: (0, 0)),
            pl.BlockSpec((copies, 1, 128), lambda j, at: (0, 0, 0)),
        ]
        scratch = [pltpu.VMEM((1, neurons), F32)]
    return pl.pallas_call(
        body,
        out_shape=out_shape,
        grid_spec=pltpu.PrefetchScalarGridSpec(
            num_scalar_prefetch=1,
            grid=(neurons // width,),
            in_specs=[
                pl.BlockSpec((rows, dim), lambda j, at: (0, 0)),
                pl.BlockSpec((rows, width), lambda j, at: (at[0], j)),
                pl.BlockSpec((width, dim), lambda j, at: (j, 0)),
            ]
            + [row]
            + [pl.BlockSpec((1, neurons), lambda j, at: (0, 0))] * len(scoring),
            out_specs=out_specs,
            scratch_shapes=scratch,
        ),
        compiler_params=params(("arbitrary",)),
        cost_estimate=pl.CostEstimate(
            flops=2 * rows * dim * neurons,
            bytes_accessed=4 * rows * neurons + 2 * weight.size,
            transcendentals=rows * neurons,
        ),
        name="score" if scoring else "readout",
    )(which_half.reshape(1), lat, in_hbm(spikes), weight, bias, *scoring)


def on_device(
    spikes,
    held_in,
    readin_weight,
    qkv_weight,
    out_weight,
    up_weight,
    down_weight,
    norm_gain,
    mlp_gain,
    final_gain,
    readout_weight,
    readout_bias,
):
    frames_all = spikes.shape[0]
    model_dim = readin_weight.shape[1]
    half = frames_all // 2
    rows_here = frames_all // lax.axis_size(ROWS)
    core = lax.axis_index("c")
    held_row = held_in[None, :]

    given, counts_far = readin(spikes, held_row, in_hbm(readin_weight), 1 - core, BF16)
    theirs = other_core(given)
    own, counts_near = readin(spikes, held_row, readin_weight, core, F32)
    chip_sum = (own + theirs.astype(F32)).astype(BF16)
    wide = ((rows_here, model_dim), BF16)
    (plane_sum,) = small(
        plane_kernel, "plane", [wide], exchange(chip_sum.reshape(16, -1, model_dim), PLANE)
    )
    (blocks,) = small(
        pair_kernel, "pair", [((16, rows_here // 4, model_dim), BF16)],
        plane_sum, other_layer(plane_sum),
    )
    parts = exchange(blocks, ("x", "zh"))

    stream, queries, kv_own = project(
        parts, norm_gain[None, :], jnp.swapaxes(qkv_weight, 0, 1), lax.axis_size(YZ)
    )
    kv_near = exchange(kv_own, YZ).reshape(half, 2 * HEAD_DIM)
    attn_parts = attend(queries, kv_near, other_core(kv_near), out_weight, lax.axis_size(TM))

    thin = (8, rows_here // 8, model_dim)
    mixed, mlp_parts = small(
        mlp_kernel, "mlp", [(thin, F32), (thin, BF16)],
        exchange(attn_parts, TM), stream, mlp_gain[None, :], up_weight, down_weight,
    )
    (own_latents,) = small(
        latents_kernel, "latents", [(thin, BF16)],
        exchange(mlp_parts, TM), mixed, final_gain[None, :], scalar=lax.axis_index(TM),
    )

    column = exchange(own_latents, ("zh", "zl")).reshape(rows_here, model_dim)
    lat_near = to_all(column, PLANE).reshape(half, model_dim)
    lat_far = other_core(lat_near)

    bias_row = readout_bias[None, :]
    (ll_near,) = readout(core, lat_near, spikes, readout_weight, bias_row)
    scoring = (ll_near, held_row, counts_near, counts_far)
    bits, sums = readout(1 - core, lat_far, spikes, readout_weight, bias_row, scoring)
    (bits_total,) = small(total_kernel, "total", [((1, 1), F32)], exchange(sums, ALL))

    out_start = lax.axis_index(ROWS) * rows_here
    out_row = lax.rem(out_start, half)
    latents = jnp.where(
        out_start // half == core,
        lax.dynamic_slice_in_dim(lat_near, out_row, rows_here, 0),
        lax.dynamic_slice_in_dim(lat_far, out_row, rows_here, 0),
    )
    return (latents, bits[0], bits_total[0, 0])


def solution(mesh):
    fine = Mesh(mesh.devices.reshape(4, 4, 2, 4, 2), ALL)
    in_specs = (
        P(None, ALL),
        P(ALL),
        P(ALL, None),
        P(None, None, TM),
        P(TM, None),
        P(None, TM),
        P(TM, None),
        P(),
        P(),
        P(),
        P(ALL, None),
        P(ALL),
    )
    out_specs = (P(ROWS, None), P(ALL), P())
    return jax.shard_map(
        on_device, mesh=fine, in_specs=in_specs, out_specs=out_specs, check_vma=False
    )
```

```python
import functools
import math

import jax
import jax.numpy as jnp
from jax import lax
from jax.experimental import pallas as pl
from jax.experimental.pallas import tpu as pltpu
from jax.sharding import Mesh
from jax.sharding import PartitionSpec as P

HEAD_DIM = 128
BF16 = jnp.bfloat16
F32 = jnp.float32
ROWS = ("y", "zh", "c")
TM = ("x", "zl")
PLANE = ("y", "x")
YZ = ("y", "zh")
ALL = ("y", "zh", "c", "x", "zl")


def normed(values, gain_vec):
    return values * lax.rsqrt(jnp.mean(values * values, -1, keepdims=True) + 1e-05) * gain_vec


def exchange(blocks, axes):
    return lax.all_to_all(blocks, axes, 0, 0, tiled=True)


def to_all(block, axes):
    return exchange(jnp.broadcast_to(block[None], (lax.axis_size(axes),) + block.shape), axes)


def other_core(block):
    return lax.ppermute(block, "c", [(0, 1), (1, 0)])


def other_layer(block):
    return lax.ppermute(block, "zl", [(0, 1), (1, 0)])


def whole(array):
    return pl.BlockSpec(array.shape, lambda *_: (0,) * array.ndim)


def in_hbm(array):
    return pltpu.with_memory_space_constraint(array, pltpu.HBM)


def params(semantics):
    return pltpu.CompilerParams(
        dimension_semantics=semantics, vmem_limit_bytes=40 * 1024 * 1024
    )


def matmul(left, right):
    return jnp.dot(left, right, preferred_element_type=F32)


def matmul_nt(left, right):
    return lax.dot_general(left, right, (((1,), (1,)), ((), ())), preferred_element_type=F32)


def readin_kernel(at_ref, spikes_ref, held_ref, weight_ref, out_ref, counts_ref):
    block = spikes_ref[...].astype(F32)
    masked = (block * held_ref[...].astype(F32)).astype(BF16)
    out_ref[...] = matmul(masked, weight_ref[...]).astype(out_ref.dtype)
    counted = jnp.sum(block, 0, keepdims=True)

    @pl.when(pl.program_id(0) == 0)
    def _():
        counts_ref[...] = counted

    @pl.when(pl.program_id(0) > 0)
    def _():
        counts_ref[...] += counted


def readin(spikes, held, weight, which_half, dtype):
    frames, neurons = spikes.shape
    dim = weight.shape[1]
    rows = frames // 4
    return pl.pallas_call(
        readin_kernel,
        out_shape=(
            jax.ShapeDtypeStruct((frames // 2, dim), dtype),
            jax.ShapeDtypeStruct((1, neurons), F32),
        ),
        grid_spec=pltpu.PrefetchScalarGridSpec(
            num_scalar_prefetch=1,
            grid=(2,),
            in_specs=[
                pl.BlockSpec((rows, neurons), lambda i, at: (2 * at[0] + i, 0)),
                pl.BlockSpec((1, neurons), lambda i, at: (0, 0)),
                pl.BlockSpec((neurons, dim), lambda i, at: (0, 0)),
            ],
            out_specs=[
                pl.BlockSpec((rows, dim), lambda i, at: (i, 0)),
                pl.BlockSpec((1, neurons), lambda i, at: (0, 0)),
            ],
        ),
        compiler_params=params(("arbitrary",)),
        cost_estimate=pl.CostEstimate(
            flops=frames * neurons * dim,
            bytes_accessed=2 * frames * neurons + 2 * neurons * dim + frames * dim,
            transcendentals=0,
        ),
        name="readin",
    )(which_half.reshape(1), in_hbm(spikes), in_hbm(held), weight)


def plane_kernel(parts_ref, out_ref):
    total = parts_ref[0].astype(F32)
    for i in range(1, parts_ref.shape[0]):
        total += parts_ref[i].astype(F32)
    out_ref[...] = total.astype(BF16)


def pair_kernel(mine_ref, other_ref, out_ref):
    total = (mine_ref[...].astype(F32) + other_ref[...].astype(F32)).astype(BF16)
    piece = out_ref.shape[1]
    for i in range(out_ref.shape[0]):
        start = piece * (i % 4)
        out_ref[i] = total[start : start + piece]


def small(body, name, out_shapes, *operands, scalar=None):
    specs = [whole(array) for array in operands]
    if scalar is not None:
        specs.insert(0, pl.BlockSpec(memory_space=pltpu.SMEM))
        operands = (scalar.reshape(1),) + operands
    return pl.pallas_call(
        body,
        out_shape=[jax.ShapeDtypeStruct(*shape) for shape in out_shapes],
        in_specs=specs,
        out_specs=[
            pl.BlockSpec(shape, lambda n=len(shape): (0,) * n) for shape, _ in out_shapes
        ],
        compiler_params=params(None),
        name=name,
    )(*operands)


def mlp_kernel(parts_ref, stream_ref, gain_ref, up_ref, down_ref, mixed_ref, out_ref):
    mixed = stream_ref[...]
    attn = parts_ref[0].astype(F32)
    for i in range(1, parts_ref.shape[0]):
        attn += parts_ref[i].astype(F32)
    mixed += attn
    mlp_in = normed(mixed, gain_ref[...]).astype(BF16)
    hidden_act = jax.nn.gelu(matmul(mlp_in, up_ref[...])).astype(BF16)
    part = matmul(hidden_act, down_ref[...])
    rows = out_ref.shape[1]
    for i in range(out_ref.shape[0]):
        mixed_ref[i] = mixed[rows * i : rows * (i + 1)]
        out_ref[i] = part[rows * i : rows * (i + 1)].astype(BF16)


def latents_kernel(at_ref, parts_ref, mixed_ref, gain_ref, out_ref):
    total = parts_ref[0].astype(F32)
    for i in range(1, parts_ref.shape[0]):
        total += parts_ref[i].astype(F32)
    own = normed(mixed_ref[at_ref[0]] + total, gain_ref[...]).astype(BF16)
    for i in range(out_ref.shape[0]):
        out_ref[i] = own


def project_kernel(parts_ref, gain_ref, weight_ref, stream_ref, queries_ref, kv_ref):
    groups = parts_ref.shape[0] // 4
    piece = parts_ref.shape[1]
    for x in range(4):
        rows = parts_ref[groups * x].astype(F32)
        for i in range(1, groups):
            rows += parts_ref[groups * x + i].astype(F32)
        stream_ref[piece * x : piece * (x + 1), :] = rows
    attn_in = normed(stream_ref[...], gain_ref[...]).astype(BF16)
    queries_ref[...] = matmul(attn_in, weight_ref[0]).astype(BF16)
    keys = matmul(attn_in, weight_ref[1]).astype(BF16)
    values = matmul(attn_in, weight_ref[2]).astype(BF16)
    for i in range(kv_ref.shape[0]):
        kv_ref[i, :, :HEAD_DIM] = keys
        kv_ref[i, :, HEAD_DIM:] = values


def project(parts, gain, weight, copies):
    rows, dim = 4 * parts.shape[1], parts.shape[2]
    shapes = ((rows, dim), F32), ((rows, HEAD_DIM), BF16), ((copies, rows, 2 * HEAD_DIM), BF16)
    return pl.pallas_call(
        project_kernel,
        out_shape=[jax.ShapeDtypeStruct(*shape) for shape in shapes],
        in_specs=[whole(array) for array in (parts, gain, weight)],
        out_specs=[
            pl.BlockSpec(shape, lambda n=len(shape): (0,) * n) for shape, _ in shapes
        ],
        compiler_params=params(None),
        name="project",
    )(parts, gain, weight)


def attend_kernel(queries_ref, near_ref, far_ref, mix_ref, out_ref):
    queries = queries_ref[...]
    numerator, denominator = 0.0, 0.0
    for kv in (near_ref, far_ref):
        scores = matmul_nt(queries, kv[:, :HEAD_DIM])
        weights = jnp.exp(scores * (1.0 / math.sqrt(HEAD_DIM)))
        numerator += matmul(weights.astype(BF16), kv[:, HEAD_DIM:])
        denominator += jnp.sum(weights, -1, keepdims=True)
    part = matmul((numerator / denominator).astype(BF16), mix_ref[...]).astype(BF16)
    for i in range(out_ref.shape[0]):
        out_ref[i] = part


def attend(queries, near, far, mix, copies):
    shape = (copies, queries.shape[0], mix.shape[1])
    operands = (queries, near, far, mix)
    return pl.pallas_call(
        attend_kernel,
        out_shape=jax.ShapeDtypeStruct(shape, BF16),
        in_specs=[whole(array) for array in operands],
        out_specs=pl.BlockSpec(shape, lambda: (0, 0, 0)),
        compiler_params=params(None),
        name="attend",
    )(*operands)


def likelihood(lat_ref, spikes_ref, weight_ref, bias_ref):
    log_rate = matmul_nt(lat_ref[...], weight_ref[...]) + bias_ref[...]
    observed = spikes_ref[...].astype(F32)
    return jnp.sum(observed * log_rate - jnp.exp(log_rate), 0, keepdims=True)


def readout_kernel(at_ref, lat, spikes, weight, bias, out):
    out[...] = likelihood(lat, spikes, weight, bias)


def score_kernel(
    frames, at_ref, lat, spikes, weight, bias, before, held, seen, seen_too, bits, sums, total
):
    step = pl.program_id(0)
    width = spikes.shape[1]
    found = likelihood(lat, spikes, weight, bias)
    for j in range(total.shape[1] // width):

        @pl.when(step == j)
        def _():
            total[:, width * j : width * (j + 1)] = found

    @pl.when(step == pl.num_programs(0) - 1)
    def _():
        heldout = (1 - held[...]).astype(F32)
        count = seen[...] + seen_too[...]
        null_ll = count * jnp.log((count + 1.0) / frames) - (count + 1.0)
        gained = heldout * (before[...] + total[...] - null_ll)
        bits[...] = gained / (math.log(2.0) * (count + 1.0))
        lane = lax.broadcasted_iota(jnp.int32, (1, 128), 1)
        gain_sum = jnp.sum(gained, 1, keepdims=True)
        spike_sum = jnp.sum(heldout * count, 1, keepdims=True)
        here = jnp.where(lane == 0, gain_sum, jnp.where(lane == 1, spike_sum, 0.0))
        sums[...] = jnp.broadcast_to(here[None], sums.shape)


def total_kernel(sums_ref, out_ref):
    totals = jnp.sum(sums_ref[...], 0)
    out_ref[...] = totals[:, 0:1] / (math.log(2.0) * (1.0 + totals[:, 1:2]))


def readout(which_half, lat, spikes, weight, bias, scoring=(), copies=256):
    frames, neurons = spikes.shape
    rows, dim = lat.shape
    width = neurons // 2
    row = pl.BlockSpec((1, width), lambda j, at: (0, j))
    out_shape, out_specs = [jax.ShapeDtypeStruct((1, neurons), F32)], [row]
    body, scratch = readout_kernel, []
    if scoring:
        body = functools.partial(score_kernel, float(frames))
        out_shape.append(jax.ShapeDtypeStruct((copies, 1, 128), F32))
        out_specs = [
            pl.BlockSpec((1, neurons), lambda j, at: (0, 0)),
            pl.BlockSpec((copies, 1, 128), lambda j, at: (0, 0, 0)),
        ]
        scratch = [pltpu.VMEM((1, neurons), F32)]
    return pl.pallas_call(
        body,
        out_shape=out_shape,
        grid_spec=pltpu.PrefetchScalarGridSpec(
            num_scalar_prefetch=1,
            grid=(neurons // width,),
            in_specs=[
                pl.BlockSpec((rows, dim), lambda j, at: (0, 0)),
                pl.BlockSpec((rows, width), lambda j, at: (at[0], j)),
                pl.BlockSpec((width, dim), lambda j, at: (j, 0)),
            ]
            + [row]
            + [pl.BlockSpec((1, neurons), lambda j, at: (0, 0))] * len(scoring),
            out_specs=out_specs,
            scratch_shapes=scratch,
        ),
        compiler_params=params(("arbitrary",)),
        cost_estimate=pl.CostEstimate(
            flops=2 * rows * dim * neurons,
            bytes_accessed=4 * rows * neurons + 2 * weight.size,
            transcendentals=rows * neurons,
        ),
        name="score" if scoring else "readout",
    )(which_half.reshape(1), lat, spikes if scoring else in_hbm(spikes), weight, bias, *scoring)


def on_device(
    spikes,
    held_in,
    readin_weight,
    qkv_weight,
    out_weight,
    up_weight,
    down_weight,
    norm_gain,
    mlp_gain,
    final_gain,
    readout_weight,
    readout_bias,
):
    frames_all = spikes.shape[0]
    model_dim = readin_weight.shape[1]
    half = frames_all // 2
    rows_here = frames_all // lax.axis_size(ROWS)
    core = lax.axis_index("c")
    held_row = held_in[None, :]

    given, counts_far = readin(spikes, held_row, in_hbm(readin_weight), 1 - core, BF16)
    theirs = other_core(given)
    own, counts_near = readin(spikes, held_row, readin_weight, core, F32)
    chip_sum = (own + theirs.astype(F32)).astype(BF16)
    wide = ((rows_here, model_dim), BF16)
    (plane_sum,) = small(
        plane_kernel, "plane", [wide], exchange(chip_sum.reshape(16, -1, model_dim), PLANE)
    )
    (blocks,) = small(
        pair_kernel, "pair", [((16, rows_here // 4, model_dim), BF16)],
        plane_sum, other_layer(plane_sum),
    )
    parts = exchange(blocks, ("x", "zh"))

    stream, queries, kv_own = project(
        parts, norm_gain[None, :], jnp.swapaxes(qkv_weight, 0, 1), lax.axis_size(YZ)
    )
    kv_near = exchange(kv_own, YZ).reshape(half, 2 * HEAD_DIM)
    attn_parts = attend(queries, kv_near, other_core(kv_near), out_weight, lax.axis_size(TM))

    thin = (8, rows_here // 8, model_dim)
    mixed, mlp_parts = small(
        mlp_kernel, "mlp", [(thin, F32), (thin, BF16)],
        exchange(attn_parts, TM), stream, mlp_gain[None, :], up_weight, down_weight,
    )
    (own_latents,) = small(
        latents_kernel, "latents", [(thin, BF16)],
        exchange(mlp_parts, TM), mixed, final_gain[None, :], scalar=lax.axis_index(TM),
    )

    column = exchange(own_latents, ("zh", "zl")).reshape(rows_here, model_dim)
    lat_near = to_all(column, PLANE).reshape(half, model_dim)
    lat_far = other_core(lat_near)

    bias_row = readout_bias[None, :]
    (ll_near,) = readout(core, lat_near, spikes, readout_weight, bias_row)
    scoring = (ll_near, held_row, counts_near, counts_far)
    bits, sums = readout(1 - core, lat_far, spikes, readout_weight, bias_row, scoring)
    (bits_total,) = small(total_kernel, "total", [((1, 1), F32)], exchange(sums, ALL))

    out_start = lax.axis_index(ROWS) * rows_here
    out_row = lax.rem(out_start, half)
    latents = jnp.where(
        out_start // half == core,
        lax.dynamic_slice_in_dim(lat_near, out_row, rows_here, 0),
        lax.dynamic_slice_in_dim(lat_far, out_row, rows_here, 0),
    )
    return (latents, bits[0], bits_total[0, 0])


def solution(mesh):
    fine = Mesh(mesh.devices.reshape(4, 4, 2, 4, 2), ALL)
    in_specs = (
        P(None, ALL),
        P(ALL),
        P(ALL, None),
        P(None, None, TM),
        P(TM, None),
        P(None, TM),
        P(TM, None),
        P(),
        P(),
        P(),
        P(ALL, None),
        P(ALL),
    )
    out_specs = (P(ROWS, None), P(ALL), P())
    return jax.shard_map(
        on_device, mesh=fine, in_specs=in_specs, out_specs=out_specs, check_vma=False
    )
```

```python
import functools
import math

import jax
import jax.numpy as jnp
from jax import lax
from jax.experimental import pallas as pl
from jax.experimental.pallas import tpu as pltpu
from jax.sharding import Mesh
from jax.sharding import PartitionSpec as P

HEAD_DIM = 128
BF16 = jnp.bfloat16
F32 = jnp.float32
ROWS = ("y", "zh", "c")
TM = ("x", "zl")
PLANE = ("y", "x")
YZ = ("y", "zh")
ALL = ("y", "zh", "c", "x", "zl")


def normed(values, gain_vec):
    return values * lax.rsqrt(jnp.mean(values * values, -1, keepdims=True) + 1e-05) * gain_vec


def exchange(blocks, axes):
    return lax.all_to_all(blocks, axes, 0, 0, tiled=True)


def to_all(block, axes):
    return exchange(jnp.broadcast_to(block[None], (lax.axis_size(axes),) + block.shape), axes)


def other_core(block):
    return lax.ppermute(block, "c", [(0, 1), (1, 0)])


def other_layer(block):
    return lax.ppermute(block, "zl", [(0, 1), (1, 0)])


def whole(array):
    return pl.BlockSpec(array.shape, lambda *_: (0,) * array.ndim)


def in_hbm(array):
    return pltpu.with_memory_space_constraint(array, pltpu.HBM)


def params(semantics):
    return pltpu.CompilerParams(
        dimension_semantics=semantics, vmem_limit_bytes=16 * 1024 * 1024
    )


def matmul(left, right):
    return jnp.dot(left, right, preferred_element_type=F32)


def matmul_nt(left, right):
    return lax.dot_general(left, right, (((1,), (1,)), ((), ())), preferred_element_type=F32)


def readin_kernel(at_ref, spikes_ref, held_ref, weight_ref, out_ref, counts_ref, seen_ref=None):
    block = spikes_ref[...].astype(F32)
    masked = (block * held_ref[...].astype(F32)).astype(BF16)
    out_ref[...] = matmul(masked, weight_ref[...]).astype(out_ref.dtype)
    counted = jnp.sum(block, 0, keepdims=True)
    if seen_ref is not None:
        seen_ref[...] = block.astype(BF16)

    @pl.when(pl.program_id(0) == 0)
    def _():
        counts_ref[...] = counted

    @pl.when(pl.program_id(0) > 0)
    def _():
        counts_ref[...] += counted


def readin(spikes, held, weight, which_half, dtype, keep=False):
    frames, neurons = spikes.shape
    dim = weight.shape[1]
    rows = frames // 4
    return pl.pallas_call(
        readin_kernel,
        out_shape=[
            jax.ShapeDtypeStruct((frames // 2, dim), dtype),
            jax.ShapeDtypeStruct((1, neurons), F32),
        ]
        + [jax.ShapeDtypeStruct((frames // 2, neurons), BF16)] * keep,
        grid_spec=pltpu.PrefetchScalarGridSpec(
            num_scalar_prefetch=1,
            grid=(2,),
            in_specs=[
                pl.BlockSpec((rows, neurons), lambda i, at: (2 * at[0] + i, 0)),
                pl.BlockSpec((1, neurons), lambda i, at: (0, 0)),
                pl.BlockSpec((neurons, dim), lambda i, at: (0, 0)),
            ],
            out_specs=[
                pl.BlockSpec((rows, dim), lambda i, at: (i, 0)),
                pl.BlockSpec((1, neurons), lambda i, at: (0, 0)),
            ]
            + [pl.BlockSpec((rows, neurons), lambda i, at: (i, 0))] * keep,
        ),
        compiler_params=params(("arbitrary",)),
        cost_estimate=pl.CostEstimate(
            flops=frames * neurons * dim,
            bytes_accessed=2 * frames * neurons + 2 * neurons * dim + frames * dim,
            transcendentals=0,
        ),
        name="readin",
    )(which_half.reshape(1), in_hbm(spikes), in_hbm(held), weight)


def plane_kernel(parts_ref, out_ref):
    total = parts_ref[0].astype(F32)
    for i in range(1, parts_ref.shape[0]):
        total += parts_ref[i].astype(F32)
    out_ref[...] = total.astype(BF16)


def pair_kernel(mine_ref, other_ref, out_ref):
    total = (mine_ref[...].astype(F32) + other_ref[...].astype(F32)).astype(BF16)
    piece = out_ref.shape[1]
    for i in range(out_ref.shape[0]):
        start = piece * (i % 4)
        out_ref[i] = total[start : start + piece]


def small(body, name, out_shapes, *operands, scalar=None):
    specs = [whole(array) for array in operands]
    if scalar is not None:
        specs.insert(0, pl.BlockSpec(memory_space=pltpu.SMEM))
        operands = (scalar.reshape(1),) + operands
    return pl.pallas_call(
        body,
        out_shape=[jax.ShapeDtypeStruct(*shape) for shape in out_shapes],
        in_specs=specs,
        out_specs=[
            pl.BlockSpec(shape, lambda n=len(shape): (0,) * n) for shape, _ in out_shapes
        ],
        compiler_params=params(None),
        name=name,
    )(*operands)


def mlp_kernel(parts_ref, stream_ref, gain_ref, up_ref, down_ref, mixed_ref, out_ref):
    mixed = stream_ref[...]
    attn = parts_ref[0].astype(F32)
    for i in range(1, parts_ref.shape[0]):
        attn += parts_ref[i].astype(F32)
    mixed += attn
    mlp_in = normed(mixed, gain_ref[...]).astype(BF16)
    hidden_act = jax.nn.gelu(matmul(mlp_in, up_ref[...])).astype(BF16)
    part = matmul(hidden_act, down_ref[...])
    rows = out_ref.shape[1]
    for i in range(out_ref.shape[0]):
        mixed_ref[i] = mixed[rows * i : rows * (i + 1)]
        out_ref[i] = part[rows * i : rows * (i + 1)].astype(BF16)


def latents_kernel(at_ref, parts_ref, mixed_ref, gain_ref, out_ref):
    total = parts_ref[0].astype(F32)
    for i in range(1, parts_ref.shape[0]):
        total += parts_ref[i].astype(F32)
    own = normed(mixed_ref[at_ref[0]] + total, gain_ref[...]).astype(BF16)
    for i in range(out_ref.shape[0]):
        out_ref[i] = own


def project_kernel(parts_ref, gain_ref, weight_ref, stream_ref, queries_ref, kv_ref):
    groups = parts_ref.shape[0] // 4
    piece = parts_ref.shape[1]
    for x in range(4):
        rows = parts_ref[groups * x].astype(F32)
        for i in range(1, groups):
            rows += parts_ref[groups * x + i].astype(F32)
        stream_ref[piece * x : piece * (x + 1), :] = rows
    attn_in = normed(stream_ref[...], gain_ref[...]).astype(BF16)
    queries_ref[...] = matmul(attn_in, weight_ref[0]).astype(BF16)
    keys = matmul(attn_in, weight_ref[1]).astype(BF16)
    values = matmul(attn_in, weight_ref[2]).astype(BF16)
    for i in range(kv_ref.shape[0]):
        kv_ref[i, :, :HEAD_DIM] = keys
        kv_ref[i, :, HEAD_DIM:] = values


def project(parts, gain, weight, copies):
    rows, dim = 4 * parts.shape[1], parts.shape[2]
    shapes = ((rows, dim), F32), ((rows, HEAD_DIM), BF16), ((copies, rows, 2 * HEAD_DIM), BF16)
    return pl.pallas_call(
        project_kernel,
        out_shape=[jax.ShapeDtypeStruct(*shape) for shape in shapes],
        in_specs=[whole(array) for array in (parts, gain, weight)],
        out_specs=[
            pl.BlockSpec(shape, lambda n=len(shape): (0,) * n) for shape, _ in shapes
        ],
        compiler_params=params(None),
        name="project",
    )(parts, gain, weight)


def attend_kernel(queries_ref, near_ref, far_ref, mix_ref, out_ref):
    queries = queries_ref[...]
    numerator, denominator = 0.0, 0.0
    for kv in (near_ref, far_ref):
        scores = matmul_nt(queries, kv[:, :HEAD_DIM])
        weights = jnp.exp(scores * (1.0 / math.sqrt(HEAD_DIM)))
        numerator += matmul(weights.astype(BF16), kv[:, HEAD_DIM:])
        denominator += jnp.sum(weights, -1, keepdims=True)
    part = matmul((numerator / denominator).astype(BF16), mix_ref[...]).astype(BF16)
    for i in range(out_ref.shape[0]):
        out_ref[i] = part


def attend(queries, near, far, mix, copies):
    shape = (copies, queries.shape[0], mix.shape[1])
    operands = (queries, near, far, mix)
    return pl.pallas_call(
        attend_kernel,
        out_shape=jax.ShapeDtypeStruct(shape, BF16),
        in_specs=[whole(array) for array in operands],
        out_specs=pl.BlockSpec(shape, lambda: (0, 0, 0)),
        compiler_params=params(None),
        name="attend",
    )(*operands)


def likelihood(lat_ref, spikes_ref, weight_ref, bias_ref):
    log_rate = matmul_nt(lat_ref[...], weight_ref[...]) + bias_ref[...]
    observed = spikes_ref[...].astype(F32)
    return jnp.sum(observed * log_rate - jnp.exp(log_rate), 0, keepdims=True)


def readout_kernel(at_ref, lat, spikes, weight, bias, out):
    out[...] = likelihood(lat, spikes, weight, bias)


def score_kernel(
    frames, at_ref, lat, spikes, weight, bias, before, held, seen, seen_too, bits, sums, total
):
    step = pl.program_id(0)
    width = spikes.shape[1]
    found = likelihood(lat, spikes, weight, bias)
    for j in range(total.shape[1] // width):

        @pl.when(step == j)
        def _():
            total[:, width * j : width * (j + 1)] = found

    @pl.when(step == pl.num_programs(0) - 1)
    def _():
        heldout = (1 - held[...]).astype(F32)
        count = seen[...] + seen_too[...]
        null_ll = count * jnp.log((count + 1.0) / frames) - (count + 1.0)
        gained = heldout * (before[...] + total[...] - null_ll)
        bits[...] = gained / (math.log(2.0) * (count + 1.0))
        lane = lax.broadcasted_iota(jnp.int32, (1, 128), 1)
        gain_sum = jnp.sum(gained, 1, keepdims=True)
        spike_sum = jnp.sum(heldout * count, 1, keepdims=True)
        here = jnp.where(lane == 0, gain_sum, jnp.where(lane == 1, spike_sum, 0.0))
        sums[...] = jnp.broadcast_to(here[None], sums.shape)


def total_kernel(sums_ref, out_ref):
    totals = jnp.sum(sums_ref[...], 0)
    out_ref[...] = totals[:, 0:1] / (math.log(2.0) * (1.0 + totals[:, 1:2]))


def readout(which_half, lat, spikes, weight, bias, scoring=(), copies=256):
    frames, neurons = spikes.shape
    rows, dim = lat.shape
    width = neurons // 2
    row = pl.BlockSpec((1, width), lambda j, at: (0, j))
    out_shape, out_specs = [jax.ShapeDtypeStruct((1, neurons), F32)], [row]
    body, scratch = readout_kernel, []
    if scoring:
        body = functools.partial(score_kernel, float(frames))
        out_shape.append(jax.ShapeDtypeStruct((copies, 1, 128), F32))
        out_specs = [
            pl.BlockSpec((1, neurons), lambda j, at: (0, 0)),
            pl.BlockSpec((copies, 1, 128), lambda j, at: (0, 0, 0)),
        ]
        scratch = [pltpu.VMEM((1, neurons), F32)]
    return pl.pallas_call(
        body,
        out_shape=out_shape,
        grid_spec=pltpu.PrefetchScalarGridSpec(
            num_scalar_prefetch=1,
            grid=(neurons // width,),
            in_specs=[
                pl.BlockSpec((rows, dim), lambda j, at: (0, 0)),
                pl.BlockSpec((rows, width), lambda j, at: (at[0], j)),
                pl.BlockSpec((width, dim), lambda j, at: (j, 0)),
            ]
            + [row]
            + [pl.BlockSpec((1, neurons), lambda j, at: (0, 0))] * len(scoring),
            out_specs=out_specs,
            scratch_shapes=scratch,
        ),
        compiler_params=params(("arbitrary",)),
        cost_estimate=pl.CostEstimate(
            flops=2 * rows * dim * neurons,
            bytes_accessed=4 * rows * neurons + 2 * weight.size,
            transcendentals=rows * neurons,
        ),
        name="score" if scoring else "readout",
    )(which_half.reshape(1), lat, spikes, weight, bias, *scoring)


def on_device(
    spikes,
    held_in,
    readin_weight,
    qkv_weight,
    out_weight,
    up_weight,
    down_weight,
    norm_gain,
    mlp_gain,
    final_gain,
    readout_weight,
    readout_bias,
):
    frames_all = spikes.shape[0]
    model_dim = readin_weight.shape[1]
    half = frames_all // 2
    rows_here = frames_all // lax.axis_size(ROWS)
    core = lax.axis_index("c")
    held_row = held_in[None, :]

    given, counts_far = readin(spikes, held_row, in_hbm(readin_weight), 1 - core, BF16)
    theirs = other_core(given)
    own, counts_near, seen_near = readin(spikes, held_row, readin_weight, core, F32, keep=True)
    chip_sum = (own + theirs.astype(F32)).astype(BF16)
    wide = ((rows_here, model_dim), BF16)
    (plane_sum,) = small(
        plane_kernel, "plane", [wide], exchange(chip_sum.reshape(16, -1, model_dim), PLANE)
    )
    (blocks,) = small(
        pair_kernel, "pair", [((16, rows_here // 4, model_dim), BF16)],
        plane_sum, other_layer(plane_sum),
    )
    parts = exchange(blocks, ("x", "zh"))

    stream, queries, kv_own = project(
        parts, norm_gain[None, :], jnp.swapaxes(qkv_weight, 0, 1), lax.axis_size(YZ)
    )
    kv_near = exchange(kv_own, YZ).reshape(half, 2 * HEAD_DIM)
    attn_parts = attend(queries, kv_near, other_core(kv_near), out_weight, lax.axis_size(TM))

    thin = (8, rows_here // 8, model_dim)
    mixed, mlp_parts = small(
        mlp_kernel, "mlp", [(thin, F32), (thin, BF16)],
        exchange(attn_parts, TM), stream, mlp_gain[None, :], up_weight, down_weight,
    )
    (own_latents,) = small(
        latents_kernel, "latents", [(thin, BF16)],
        exchange(mlp_parts, TM), mixed, final_gain[None, :], scalar=lax.axis_index(TM),
    )

    column = exchange(own_latents, ("zh", "zl")).reshape(rows_here, model_dim)
    lat_near = to_all(column, PLANE).reshape(half, model_dim)
    lat_far = other_core(lat_near)

    bias_row = readout_bias[None, :]
    (ll_near,) = readout(jnp.int32(0), lat_near, in_hbm(seen_near), readout_weight, bias_row)
    scoring = (ll_near, held_row, counts_near, counts_far)
    bits, sums = readout(1 - core, lat_far, spikes, readout_weight, bias_row, scoring)
    (bits_total,) = small(total_kernel, "total", [((1, 1), F32)], exchange(sums, ALL))

    out_start = lax.axis_index(ROWS) * rows_here
    out_row = lax.rem(out_start, half)
    latents = jnp.where(
        out_start // half == core,
        lax.dynamic_slice_in_dim(lat_near, out_row, rows_here, 0),
        lax.dynamic_slice_in_dim(lat_far, out_row, rows_here, 0),
    )
    return (latents, bits[0], bits_total[0, 0])


def solution(mesh):
    fine = Mesh(mesh.devices.reshape(4, 4, 2, 4, 2), ALL)
    in_specs = (
        P(None, ALL),
        P(ALL),
        P(ALL, None),
        P(None, None, TM),
        P(TM, None),
        P(None, TM),
        P(TM, None),
        P(),
        P(),
        P(),
        P(ALL, None),
        P(ALL),
    )
    out_specs = (P(ROWS, None), P(ALL), P())
    return jax.shard_map(
        on_device, mesh=fine, in_specs=in_specs, out_specs=out_specs, check_vma=False
    )
```
